32 devices in a mesh: rollout: 2 (over y), branch: 4 (over z), seq: 4 (over x, core).
Axes of the slice: x: 2, y: 2, z: 4, core: 2. Of those that a mesh axis runs over, the one named last changes fastest.
Arguments:
- queries: bfloat16 [8, 512, 4096], P(('rollout', 'branch'), 'seq'), parts along dimension 0, may hold values from -8 to 8
- keyvals: bfloat16 [8, 512, 2, 256], P(('rollout', 'branch'), 'seq'), parts along dimension 0, may hold values from -4 to 4
- residual: bfloat16 [8, 512, 4096], P(('rollout', 'branch'), 'seq'), parts along dimension 0, may hold values from -3 to 3
- read_list: int32 [8, 4, 3], P(('rollout', 'branch'), 'seq'), parts along dimension 0, may hold values from 0 to 3
- router: bfloat16 [4096, 8], replicated, may hold values from -0.09375 to 0.09375
- expert_ids: int32 [8, 512, 2], P(('rollout', 'branch'), 'seq'), parts along dimension 0, may hold values from 0 to 7, all different within a row; in each aligned block of 128 rows (0 to 127, 128 to 255, ..., all dimensions but the last counted through in order) at most 48 rows name the same one
- w_gate_up: bfloat16 [16, 4096, 2, 384], P(('branch', 'seq')), may hold values from -0.09375 to 0.09375
- w_down: bfloat16 [16, 384, 4096], P(('branch', 'seq')), may hold values from -0.21875 to 0.21875
Outputs:
- mixed: bfloat16 [8, 512, 4096], P(('rollout', 'branch'), 'seq'), parts along dimension 0
The draws below stay inside these ranges and needn't reach their ends.
There are 2 independent parts, one for each index of `rollout`. The reference program is written for one: setup_inputs(seed, part) draws one part's arguments, and reference() takes and returns one part's arrays. A program takes and returns all parts, laid end to end along the dimension named above; an argument that names none is the same for every part. Nothing has to cross between parts.
Inputs may be any that keep to these rules, and one draw needn't show every extreme that they name: read_list[c, s, o] is the block of branch c that query block s of branch (c + o + 1) mod 4 reads. `expert_ids`: each token names 2 different experts; of the 128 tokens of one device at most 48 name one expert, and in every draw some expert is named by exactly 48 tokens of some device.
All inputs are finite; a program needn't handle non-finite values.
Results may differ from the reference program's by a relative error of at most 0.0062.
Values may be sent and summed in bfloat16 or wider, within the bound.
A program may use at most 192 MiB of HBM per device.

```python
import math
import jax
import jax.numpy as jnp
import numpy as np
from jax import lax

D = 4096
HEAD_SIZE = 128
QUERY_HEADS = 32
KEY_VALUE_HEADS = 2
FF = 768
TOP = 2
TOK_DEV = 128
SIBLING_COUNT = 4
NBLK = 4
SUFFIX_LENGTH = 512
EXPERTS = 8
CAP = 48
N_BRANCH = 4
N_SEQ = 4


def draw_queries(key, part):
    complete_shape = (SIBLING_COUNT, SUFFIX_LENGTH, QUERY_HEADS * HEAD_SIZE)
    drawn = jnp.clip(2.0 * jax.random.normal(jax.random.fold_in(key, 11), complete_shape, jnp.float32), -8.0, 8.0)
    return drawn.astype(jnp.bfloat16)


def draw_keyvals(key, part):
    complete_shape = (SIBLING_COUNT, SUFFIX_LENGTH, 2, KEY_VALUE_HEADS * HEAD_SIZE)
    drawn = jnp.clip(jax.random.normal(jax.random.fold_in(key, 21), complete_shape, jnp.float32), -4.0, 4.0)
    return drawn.astype(jnp.bfloat16)


def plant(values, stream_key, least, top_value):
    longest = values.shape.index(max(values.shape))
    spots = []
    for shift in (0, 1):
        where = [jax.random.randint(jax.random.fold_in(stream_key, axis), (), 0, length) for axis, length in enumerate(values.shape)]
        where[longest] = (where[longest] + shift) % values.shape[longest]
        spots.append(tuple(where))
    return values.at[spots[0]].set(least).at[spots[1]].set(top_value)


def levels(stream_key, extent, shards, smallest, top_value):
    gain = 1.0
    for position, parts in shards:
        heights = jax.random.uniform(jax.random.fold_in(jax.random.fold_in(stream_key, 6), position), (parts,), jnp.float32, smallest / len(shards), top_value / len(shards))
        gain = gain * jnp.repeat(jnp.exp(heights), extent[position] // parts).reshape((-1,) + (1,) * (len(extent) - 1 - position))
    return gain


def deal_out(own_key, own, number, rows, amount, top, limit, lean):
    sequence = jax.random.permutation(own_key, amount)
    crowded, common = shares(amount, rows * top, limit, lean, True), shares(amount, rows * top, limit, lean, False)
    places = jnp.arange(amount)

    def named(tallies, turn):
        used = int((tallies > 0).sum())
        fixed = max(1, used // 4)
        moved = fixed + (places - fixed + turn * (used - fixed)) % max(1, amount - fixed)
        return jnp.zeros((amount,), jnp.int32).at[sequence[jnp.where(places < fixed, places, moved)]].set(jnp.asarray(tallies, jnp.int32))

    tallies = jnp.where(number % 4 == 0, named(crowded, number // 4), named(common, number - number // 4 - 1))
    mixed = jax.random.permutation(jax.random.fold_in(own, 3), amount)
    donor, taker = mixed[0:amount // 2 * 2:2], mixed[1:amount // 2 * 2:2]
    margin = jnp.minimum(tallies[donor] - 1, limit - tallies[taker]) // 2
    margin = jnp.where((donor == sequence[0]) | (taker == sequence[0]) | (tallies[taker] == 0), 0, jnp.maximum(margin, 0))
    moved = jax.random.randint(jax.random.fold_in(own, 4), (amount // 2,), 0, 1 << 20) % (margin + 1)
    tallies = tallies.at[donor].add(-moved).at[taker].add(moved)
    members = jnp.searchsorted(jnp.cumsum(tallies), jnp.arange(rows * top), side="right").astype(jnp.int32)
    grid = members.reshape(top, rows).T
    grid = grid[jax.random.permutation(jax.random.fold_in(own, 1), rows)]
    turn = jax.random.randint(jax.random.fold_in(own, 2), (rows, 1), 0, top)
    return jnp.take_along_axis(grid, (jnp.arange(top)[None, :] + turn) % top, axis=1)


def shares(count, total, bound, skew, full):
    weights = [(1 << 20) // math.isqrt(standing ** skew) + 1 for standing in range(1, count + 1)]
    largest = bound if full else min(bound, max(-(-total // count), total * weights[0] // sum(weights)))
    least = 1 if total - largest >= count - 1 else 0
    given, surplus = [largest] + [least] * (count - 1), total - largest - least * (count - 1)
    while surplus > 0:
        free = [i for i in range(1, count) if given[i] < largest] or [i for i in range(1, count) if given[i] < bound]
        mass, budget = sum([weights[i] for i in free]), surplus
        for i in free:
            extra = min(bound - given[i], max(1, budget * weights[i] // mass), surplus)
            given[i] = given[i] + extra
            surplus = surplus - extra
    return np.array(given)


def bell_draw(key, shape, scale, reach, cuts=(), kind=jnp.bfloat16):
    entries = scale * jax.random.normal(key, shape, jnp.float32)
    if cuts:
        entries = entries * levels(key, shape, cuts, -0.22, 0.18)
    return jnp.clip(entries, -reach, reach).astype(kind)


def setup_inputs(seed: int = 0, part: int = 0) -> dict:
    key_of = jax.random.split(jax.random.key(seed), 9)
    part_splits = jax.random.split(jax.random.fold_in(key_of[8], part), 9)
    queries = draw_queries(jax.random.fold_in(jax.random.fold_in(key_of[8], part), 71), part)
    keyvals = draw_keyvals(jax.random.fold_in(jax.random.fold_in(key_of[8], part), 71), part)
    residual = bell_draw(part_splits[2], (SIBLING_COUNT, SUFFIX_LENGTH, D), 0.5, 3.0, ((0, 4), (1, 4)))
    read_list = plant(jax.random.randint(part_splits[3], (SIBLING_COUNT, NBLK, SIBLING_COUNT - 1), 0, NBLK), jax.random.fold_in(part_splits[3], 1), 0, NBLK - 1).astype(jnp.int32)
    router = bell_draw(key_of[4], (D, EXPERTS), D ** -0.5, 0.09375)
    expert_ids_keys = jax.random.split(jax.random.fold_in(part_splits[5], 1), SIBLING_COUNT * SUFFIX_LENGTH // TOK_DEV)
    expert_ids_turns = jax.random.permutation(jax.random.fold_in(part_splits[5], 3), SIBLING_COUNT * SUFFIX_LENGTH // TOK_DEV)
    expert_ids = jax.vmap(lambda own, number: deal_out(jax.random.fold_in(part_splits[5], 2), own, number, TOK_DEV, EXPERTS, TOP, CAP, 2))(expert_ids_keys, expert_ids_turns).reshape((SIBLING_COUNT, SUFFIX_LENGTH, TOP))
    w_gate_up = bell_draw(key_of[6], (2 * EXPERTS, D, 2, FF // 2), D ** -0.5, 0.09375, ((0, 16),))
    w_down = bell_draw(key_of[7], (2 * EXPERTS, FF // 2, D), FF ** -0.5, 0.21875, ((0, 16),))
    return {"queries": queries, "keyvals": keyvals, "residual": residual, "read_list": read_list, "router": router, "expert_ids": expert_ids, "w_gate_up": w_gate_up, "w_down": w_down}


def attend_block(q_rows, own_kv, sib_kv, block_index):
    block_len = q_rows.shape[0]
    length_own = own_kv.shape[0]
    positions = block_index * block_len + jnp.arange(block_len, dtype=jnp.int32)
    own_allowed = jnp.arange(length_own, dtype=jnp.int32)[None, :] <= positions[:, None]
    allowed = jnp.concatenate([own_allowed, jnp.ones((block_len, sib_kv.shape[0]), dtype=bool)], axis=1)
    key_rows = jnp.concatenate([own_kv[:, 0], sib_kv[:, 0]], axis=0).astype(jnp.float32)
    value_rows = jnp.concatenate([own_kv[:, 1], sib_kv[:, 1]], axis=0).astype(jnp.float32)
    group_count = QUERY_HEADS // KEY_VALUE_HEADS
    inv_scale = 1.0 / math.sqrt(HEAD_SIZE)
    pieces = []
    for head_key_value in range(KEY_VALUE_HEADS):
        key_head = key_rows[:, head_key_value * HEAD_SIZE:(head_key_value + 1) * HEAD_SIZE]
        value_head = value_rows[:, head_key_value * HEAD_SIZE:(head_key_value + 1) * HEAD_SIZE]
        query_head = q_rows[:, head_key_value * group_count * HEAD_SIZE:(head_key_value + 1) * group_count * HEAD_SIZE]
        query_head = query_head.reshape(block_len, group_count, HEAD_SIZE).astype(jnp.float32)
        scores = jnp.einsum('tgd,kd->gtk', query_head, key_head) * inv_scale
        scores = jnp.where(allowed[None], scores, -1e+30)
        row_max = lax.optimization_barrier(jnp.max(scores, axis=-1, keepdims=True))
        expterm = jnp.exp(scores - row_max)
        probs = (expterm / lax.optimization_barrier(jnp.sum(expterm, axis=-1, keepdims=True))).astype(jnp.bfloat16)
        mixture = jnp.einsum('gtk,kd->tgd', probs.astype(jnp.float32), value_head)
        pieces.append(mixture.reshape(block_len, group_count * HEAD_SIZE))
    return jnp.concatenate(pieces, axis=1).astype(jnp.bfloat16)

def reference(queries, keyvals, residual, read_list, router, expert_ids, w_gate_up, w_down):
    block_len = TOK_DEV
    kv_width = keyvals.shape[-1]
    blocks = keyvals.reshape(SIBLING_COUNT, NBLK, block_len, 2, kv_width)

    def one_block(block_item):
        branch = block_item // NBLK
        block_at = block_item % NBLK
        others = ((branch + 1 + jnp.arange(SIBLING_COUNT - 1, dtype=jnp.int32)) % SIBLING_COUNT).astype(jnp.int32)
        offset = ((branch - others - 1) % SIBLING_COUNT).astype(jnp.int32)
        chosen = read_list[others, block_at, offset].astype(jnp.int32)
        sibling = blocks[others, chosen].reshape((SIBLING_COUNT - 1) * block_len, 2, kv_width)
        own_kv = keyvals[branch]
        q_rows = lax.dynamic_slice_in_dim(queries[branch], (block_at * block_len).astype(jnp.int32), block_len, 0)
        return attend_block(q_rows, own_kv, sibling, block_at)
    context = lax.map(one_block, jnp.arange(SIBLING_COUNT * NBLK, dtype=jnp.int32))
    context = context.reshape(SIBLING_COUNT, SUFFIX_LENGTH, QUERY_HEADS * HEAD_SIZE)
    state = residual.astype(jnp.float32) + context.astype(jnp.float32)
    normed = (state * lax.rsqrt(lax.optimization_barrier(jnp.mean(state * state, axis=-1, keepdims=True)) + 1e-06)).astype(jnp.bfloat16)
    flat_rows = normed.reshape(-1, D)
    logits = jnp.dot(flat_rows, router, preferred_element_type=jnp.float32)
    routed = expert_ids.reshape(-1, TOP).astype(jnp.int32)
    chosen_logits = jnp.take_along_axis(logits, routed, axis=1)
    gate_mix = 1.0 / lax.optimization_barrier(jnp.sum(jnp.exp(chosen_logits[:, None, :] - chosen_logits[:, :, None]), axis=-1))
    flat_ids = routed.reshape(-1)
    rows_total = flat_ids.shape[0]
    most_rows = N_BRANCH * N_SEQ * CAP
    paired = w_gate_up.reshape(EXPERTS, 2, D, 2, FF // 2)
    down_pairs = w_down.reshape(EXPERTS, 2, FF // 2, D)

    def one_expert(expert, out_table):
        row_at = jnp.nonzero(flat_ids == expert, size=most_rows, fill_value=rows_total)[0].astype(jnp.int32)
        token_at = jnp.minimum(row_at, rows_total - 1) // TOP
        expert_rows = flat_rows[token_at]
        pair_now = paired[expert]
        gate_cols = jnp.concatenate([pair_now[0, :, 0], pair_now[1, :, 0]], axis=1)
        up_cols = jnp.concatenate([pair_now[0, :, 1], pair_now[1, :, 1]], axis=1)
        down_rows = jnp.concatenate([down_pairs[expert, 0], down_pairs[expert, 1]], axis=0)
        gate_val = jnp.dot(expert_rows, gate_cols, preferred_element_type=jnp.float32)
        up_val = jnp.dot(expert_rows, up_cols, preferred_element_type=jnp.float32)
        hidden_act = (jax.nn.silu(gate_val) * up_val).astype(jnp.bfloat16)
        outputs = jnp.dot(hidden_act, down_rows, preferred_element_type=jnp.float32).astype(jnp.bfloat16)
        return out_table.at[row_at].set(outputs, mode='drop')
    out_table = jnp.zeros((rows_total, D), jnp.bfloat16)
    out_table = lax.fori_loop(0, EXPERTS, one_expert, out_table)
    expert_out = out_table.reshape(-1, TOP, D)
    layer_out = state.reshape(-1, D)
    for slot_k in range(TOP):
        layer_out = layer_out + gate_mix[:, slot_k:slot_k + 1] * expert_out[:, slot_k].astype(jnp.float32)
    return layer_out.reshape(SIBLING_COUNT, SUFFIX_LENGTH, D).astype(jnp.bfloat16)
```

```python
import functools
import math

import jax
import jax.numpy as jnp
from jax import lax
from jax.experimental import pallas as pl
from jax.experimental.pallas import tpu as pltpu
from jax.sharding import PartitionSpec as P

HEAD_SIZE = 128
PARTS = 4
CHUNKS = 4
VMEM_LIMIT = 60 * 1024 * 1024
F32 = jnp.float32
BF16 = jnp.bfloat16
ANY = pl.BlockSpec(memory_space=pl.ANY)
VMEM = pl.BlockSpec(memory_space=pltpu.VMEM)
SMEM = pl.BlockSpec(memory_space=pltpu.SMEM)


def flipped(number, mask, count):
    value, bit = 0, 1
    while bit < count:
        value = value + ((number // bit + mask // bit) % 2) * bit
        bit *= 2
    return value


def attend_kernel(
    experts, cap, n_branch, n_seq,
    list_ref, q_ref, own_ref, res_ref, router_ref, ids_ref, idt_ref,
    send_ref, state_ref, gate_ref, norm_ref, meta_ref,
    picked, sib_ref, tops, totals, ssem, rsem,
):
    branch = lax.axis_index("branch")
    seq = lax.axis_index("seq")
    me = (branch * n_seq + seq) // 2
    rows, width = q_ref.shape
    kv_heads = own_ref.shape[2] // (2 * HEAD_SIZE)
    group = width // HEAD_SIZE // kv_heads
    together = 2
    tall = together * rows
    own_len = n_seq * rows
    sib_len = (n_branch - 1) * rows
    scale = 1.0 / math.sqrt(HEAD_SIZE)
    nt = (((1,), (1,)), ((), ()))

    barrier = pltpu.get_barrier_semaphore()
    for step in range(1, n_branch):
        pl.semaphore_signal(
            barrier, inc=1, device_id={"branch": (branch + step) % n_branch},
            device_id_type=pl.DeviceIdType.MESH,
        )
    for offset in range(n_branch - 1):
        picked[offset] = own_ref[(seq - list_ref[offset] + n_seq) % n_seq]
    pl.semaphore_wait(barrier, n_branch - 1)
    copies = []
    for offset in range(n_branch - 1):
        copy = pltpu.make_async_remote_copy(
            src_ref=picked.at[offset], dst_ref=sib_ref.at[offset],
            send_sem=ssem.at[offset], recv_sem=rsem.at[offset],
            device_id={"branch": (branch + offset + 1) % n_branch},
            device_id_type=pl.DeviceIdType.MESH,
        )
        copy.start()
        copies.append(copy)

    at_row = lax.broadcasted_iota(jnp.int32, (tall, own_len), 0) % rows
    at_col = lax.broadcasted_iota(jnp.int32, (tall, own_len), 1)
    earlier = at_col // rows
    bias = jnp.where(
        earlier == 0,
        jnp.where(at_col <= at_row, 0.0, -1e30),
        jnp.where(earlier <= seq, 0.0, -1e30),
    )

    def head_parts(head, step):
        base = (head * group + step * together) * HEAD_SIZE
        cols = [
            pl.ds(pl.multiple_of(base + i * HEAD_SIZE, HEAD_SIZE), HEAD_SIZE)
            for i in range(together)
        ]
        return cols, jnp.concatenate([q_ref[:, c] for c in cols], axis=0)

    def kv_cols(head):
        return (
            slice(head * HEAD_SIZE, (head + 1) * HEAD_SIZE),
            slice((kv_heads + head) * HEAD_SIZE, (kv_heads + head + 1) * HEAD_SIZE),
        )

    steps = group // together
    for head in range(kv_heads):
        kcol, vcol = kv_cols(head)

        @pl.loop(0, steps)
        def _(step):
            cols, q = head_parts(head, step)
            keys = own_ref[:, :, kcol].reshape(own_len, HEAD_SIZE)
            values = own_ref[:, :, vcol].reshape(own_len, HEAD_SIZE)
            scores = lax.dot_general(q, keys, nt, preferred_element_type=F32) * scale + bias
            top = jnp.max(scores, axis=1, keepdims=True)
            p = jnp.exp(scores - top)
            tops[head * steps + step] = top
            totals[head * steps + step] = jnp.sum(p, axis=1, keepdims=True)
            mixed = jnp.dot(p.astype(BF16), values, preferred_element_type=F32)
            for i, c in enumerate(cols):
                state_ref[:, c] = mixed[i * rows : (i + 1) * rows]

    for copy in copies:
        copy.wait()
    for head in range(kv_heads):
        kcol, vcol = kv_cols(head)

        @pl.loop(0, steps)
        def _(step):
            cols, q = head_parts(head, step)
            keys = sib_ref[:, :, kcol].reshape(sib_len, HEAD_SIZE)
            values = sib_ref[:, :, vcol].reshape(sib_len, HEAD_SIZE)
            scores = lax.dot_general(q, keys, nt, preferred_element_type=F32) * scale
            own_top = tops[head * steps + step]
            top = jnp.maximum(own_top, jnp.max(scores, axis=1, keepdims=True))
            p = jnp.exp(scores - top)
            shrink = jnp.exp(own_top - top)
            total = totals[head * steps + step] * shrink + jnp.sum(p, axis=1, keepdims=True)
            mixed = jnp.dot(p.astype(BF16), values, preferred_element_type=F32)
            inverse = 1.0 / total
            for i, c in enumerate(cols):
                part = slice(i * rows, (i + 1) * rows)
                context = (state_ref[:, c] * shrink[part] + mixed[part]) * inverse[part]
                state_ref[:, c] = res_ref[:, c].astype(F32) + context.astype(BF16).astype(F32)

    state = state_ref[...]
    normed = (
        state * lax.rsqrt(jnp.mean(state * state, axis=1, keepdims=True) + 1e-06)
    ).astype(BF16)
    logits = lax.dot_general(normed, router_ref[...], nt, preferred_element_type=F32)

    top_count = ids_ref.shape[1]
    ids, idt = ids_ref[...], idt_ref[...]
    kinds = lax.broadcasted_iota(jnp.int32, (rows, experts), 1)
    kinds_t = lax.broadcasted_iota(jnp.int32, (experts, rows), 0)
    hot = [(ids[:, k : k + 1] == kinds).astype(F32) for k in range(top_count)]
    hot_t = [(idt[k : k + 1, :] == kinds_t).astype(F32) for k in range(top_count)]
    down = lax.broadcasted_iota(jnp.int32, (rows, rows), 0)
    along = lax.broadcasted_iota(jnp.int32, (rows, rows), 1)
    before = jnp.dot((along < down).astype(F32).astype(BF16), sum(hot).astype(BF16), preferred_element_type=F32)
    before_t = jnp.dot(sum(hot_t).astype(BF16), (down < along).astype(F32).astype(BF16), preferred_element_type=F32)
    dest, dest_t = [], []
    for k in range(top_count):
        slot = jnp.sum(before * hot[k], axis=1, keepdims=True).astype(jnp.int32)
        dest.append((ids[:, k : k + 1] ^ me) * cap + slot)
        slot_t = jnp.sum(before_t * hot_t[k], axis=0, keepdims=True).astype(jnp.int32)
        dest_t.append((idt[k : k + 1, :] ^ me) * cap + slot_t)
    chosen = [jnp.sum(logits * hot[k], axis=1, keepdims=True) for k in range(top_count)]
    gates = [1.0 / sum(jnp.exp(c - chosen[k]) for c in chosen) for k in range(top_count)]

    parts, _, part_width = norm_ref.shape
    for c in range(parts):
        norm_ref[c] = normed[:, c * part_width : (c + 1) * part_width]
    logits_t = lax.dot_general(router_ref[...], normed, nt, preferred_element_type=F32)
    chosen_t = [jnp.sum(logits_t * hot_t[k], axis=0, keepdims=True) for k in range(top_count)]
    meta_ref[...] = jnp.zeros_like(meta_ref)
    for k in range(top_count):
        meta_ref[k : k + 1, :] = dest_t[k].astype(F32)
        meta_ref[top_count + k : top_count + k + 1, :] = 1.0 / sum(
            jnp.exp(c - chosen_t[k]) for c in chosen_t
        )

    pair = 2 * cap
    places = lax.broadcasted_iota(jnp.int32, (rows, pair), 1)
    places_t = lax.broadcasted_iota(jnp.int32, (pair, rows), 0)
    for p in range(send_ref.shape[0] // pair):
        pick = sum((dest_t[k] - p * pair == places_t).astype(F32) for k in range(top_count))
        send_ref[p * pair : (p + 1) * pair, :] = jnp.dot(
            pick.astype(BF16), normed, preferred_element_type=F32
        ).astype(BF16)
        weight = sum(
            jnp.where(dest[k] - p * pair == places, gates[k], 0.0) for k in range(top_count)
        )
        high = weight.astype(BF16)
        gate_ref[p, 0] = high
        gate_ref[p, 1] = (weight - high.astype(F32)).astype(BF16)


def attend(listed, q, own, residual, router_t, ids, experts, near, cap, n_branch, n_seq):
    rows, width = q.shape
    halves = width // HEAD_SIZE // 2
    return pl.pallas_call(
        functools.partial(attend_kernel, experts, cap, n_branch, n_seq),
        out_shape=(
            jax.ShapeDtypeStruct((near * cap, width), BF16),
            jax.ShapeDtypeStruct((rows, width), F32),
            jax.ShapeDtypeStruct((near // 2, 2, rows, 2 * cap), BF16),
            jax.ShapeDtypeStruct((PARTS, rows, width // PARTS), BF16),
            jax.ShapeDtypeStruct((8, rows), F32),
        ),
        in_specs=[SMEM] + [VMEM] * 6,
        out_specs=(VMEM,) * 5,
        scratch_shapes=[
            pltpu.VMEM((n_branch - 1, rows, own.shape[2]), BF16),
            pltpu.VMEM((n_branch - 1, rows, own.shape[2]), BF16),
            pltpu.VMEM((halves, 2 * rows, 1), F32),
            pltpu.VMEM((halves, 2 * rows, 1), F32),
            pltpu.SemaphoreType.DMA((n_branch,)),
            pltpu.SemaphoreType.DMA((n_branch,)),
        ],
        compiler_params=pltpu.CompilerParams(
            collective_id=0, has_side_effects=True, vmem_limit_bytes=VMEM_LIMIT
        ),
    )(listed, q, own, residual, router_t, ids, ids.T)


def expert_kernel(
    experts, cap, n_seq,
    send_ref, state_ref, gate_ref, wgu_ref, wdn_ref, out_ref,
    recv, res, ret, wgu, wdn, acc,
    wsend, wrecv, wloc, lsem, dsend, drecv, bsend, brecv,
):
    branch = lax.axis_index("branch")
    seq = lax.axis_index("seq")
    core = seq % 2
    me = (branch * n_seq + seq) // 2
    pair = 2 * cap
    width = send_ref.shape[1]
    twin = {"seq": seq + 1 - 2 * core}
    mesh_id = pl.DeviceIdType.MESH

    def place(k):
        other = flipped(me, k, experts)
        return {"branch": (2 * other) // n_seq, "seq": (2 * other) % n_seq + core}

    barrier = pltpu.get_barrier_semaphore()
    pl.semaphore_signal(barrier, inc=1, device_id=twin, device_id_type=mesh_id)

    @pl.loop(1, experts)
    def _(k):
        pl.semaphore_signal(barrier, inc=1, device_id=place(k), device_id_type=mesh_id)

    pl.semaphore_wait(barrier, experts)

    def block(k):
        return pl.ds(pl.multiple_of(k * cap, 16), cap)

    def dispatch(k):
        return pltpu.make_async_remote_copy(
            src_ref=send_ref.at[block(k)], dst_ref=recv.at[block(k)],
            send_sem=dsend.at[k], recv_sem=drecv.at[k],
            device_id=place(k), device_id_type=mesh_id,
        )

    def give_back(k):
        return pltpu.make_async_remote_copy(
            src_ref=res.at[block(k)], dst_ref=ret.at[block(k)],
            send_sem=bsend.at[k], recv_sem=brecv.at[k],
            device_id=place(k), device_id_type=mesh_id,
        )

    weights = []
    for i, (src, dst) in enumerate(((wgu_ref, wgu), (wdn_ref, wdn))):
        weights.append(
            pltpu.make_async_remote_copy(
                src_ref=src, dst_ref=dst.at[1], send_sem=wsend.at[i], recv_sem=wrecv.at[i],
                device_id=twin, device_id_type=mesh_id,
            )
        )
        weights.append(pltpu.make_async_copy(src, dst.at[0], wloc.at[i]))
    dispatch(1).start()
    mine = pltpu.make_async_copy(send_ref.at[block(0)], recv.at[block(0)], lsem)
    mine.start()

    @pl.loop(experts // 2, experts)
    def _(k):
        dispatch(k).start()

    @pl.loop(2, experts // 2)
    def _(k):
        dispatch(k).start()

    for copy in weights:
        copy.start()
    acc[...] = state_ref[...]
    for copy in weights:
        copy.wait()

    chunk = 512

    def compute(p):
        span = pl.ds(pl.multiple_of(p * pair, 16), pair)
        acts = []
        for h in range(2):
            x = recv[span, :]
            gate = jnp.dot(x, wgu[h, 0], preferred_element_type=F32)
            up = jnp.dot(x, wgu[h, 1], preferred_element_type=F32)
            acts.append((gate / (1.0 + jnp.exp(-gate)) * up).astype(BF16))
        for start in range(0, width, chunk):
            cols = slice(start, start + chunk)
            done = jnp.dot(acts[0], wdn[0, :, cols], preferred_element_type=F32)
            done += jnp.dot(acts[1], wdn[1, :, cols], preferred_element_type=F32)
            res[span, cols] = done.astype(BF16)

    quarter = experts // 4

    def turn(i):
        return jnp.where(i <= quarter, i + quarter - 1, i - quarter)

    mine.wait()
    dispatch(1).wait_recv()
    compute(0)
    give_back(1).start()

    @pl.loop(1, experts // 2)
    def _(i):
        p = turn(i)
        dispatch(2 * p).wait_recv()
        dispatch(2 * p + 1).wait_recv()
        compute(p)
        give_back(2 * p).start()
        give_back(2 * p + 1).start()

    def add(p, rows):
        for start in range(0, width, chunk):
            cols = slice(start, start + chunk)
            block_rows = rows(cols)
            acc[:, cols] += jnp.dot(
                gate_ref[p, 0], block_rows, preferred_element_type=F32
            ) + jnp.dot(gate_ref[p, 1], block_rows, preferred_element_type=F32)

    give_back(1).wait_recv()
    add(0, lambda cols: jnp.concatenate([res[0:cap, cols], ret[cap:pair, cols]], axis=0))

    @pl.loop(1, experts // 2)
    def _(i):
        p = turn(i)
        give_back(2 * p).wait_recv()
        give_back(2 * p + 1).wait_recv()
        span = pl.ds(pl.multiple_of(p * pair, 16), pair)
        add(p, lambda cols: ret[span, cols])

    out_ref[...] = acc[...].astype(BF16)

    @pl.loop(1, experts)
    def _(k):
        dispatch(k).wait_send()
        give_back(k).wait_send()


def run_experts(send, state, gate, wgu, wdn, experts, cap, n_seq):
    rows, width = state.shape
    ff = wdn.shape[0]
    return pl.pallas_call(
        functools.partial(expert_kernel, experts, cap, n_seq),
        out_shape=jax.ShapeDtypeStruct((rows, width), BF16),
        in_specs=[ANY, VMEM, VMEM, ANY, ANY],
        out_specs=VMEM,
        scratch_shapes=[
            pltpu.VMEM((experts * cap, width), BF16),
            pltpu.VMEM((experts * cap, width), BF16),
            pltpu.VMEM((experts * cap, width), BF16),
            pltpu.VMEM((2, 2, width, ff), BF16),
            pltpu.VMEM((2, ff, width), BF16),
            pltpu.VMEM((rows, width), F32),
            pltpu.SemaphoreType.DMA((2,)),
            pltpu.SemaphoreType.DMA((2,)),
            pltpu.SemaphoreType.DMA((2,)),
            pltpu.SemaphoreType.DMA,
            pltpu.SemaphoreType.DMA((experts,)),
            pltpu.SemaphoreType.DMA((experts,)),
            pltpu.SemaphoreType.DMA((experts,)),
            pltpu.SemaphoreType.DMA((experts,)),
        ],
        compiler_params=pltpu.CompilerParams(
            collective_id=1, has_side_effects=True, vmem_limit_bytes=VMEM_LIMIT
        ),
    )(send, state, gate, wgu, wdn)


def line_kernel(
    experts, cap, n_branch, n_seq,
    list_ref, q_ref, kv_ref, res_ref, router_ref, idt_ref, wgu_ref, wdn_ref,
    out_ref,
    own, picked, sib, tops, totals, state, norm, raw, meta, xmeta,
    recv, res, back, fwd, wgu, wdn, xout, fin,
    kloc, ksend, krecv, ssend, srecv, wsend, wrecv, wloc,
    rowsend, rowrecv, relsend, relrecv, msend, mrecv,
    fsend, drecv, bsend, brecv, osend, orecv,
):
    branch = lax.axis_index("branch")
    seq = lax.axis_index("seq")
    inner = (branch + 1) // 2 % 2
    mesh_id = pl.DeviceIdType.MESH
    rows, width = q_ref.shape
    kv_heads = own.shape[2] // (2 * HEAD_SIZE)
    group = width // HEAD_SIZE // kv_heads
    own_len = n_seq * rows
    sib_len = (n_branch - 1) * rows
    scale = 1.0 / math.sqrt(HEAD_SIZE)
    nt = (((1,), (1,)), ((), ()))
    step = width // PARTS
    span = rows // CHUNKS
    pack = 2 * rows // span
    halves = group // pack

    across = (seq + 2) % n_seq
    near = branch + 1 - 2 * (branch % 2)
    far = n_branch - 1 - branch
    onward = near + inner * (far - near)
    places = [
        {"branch": branch, "seq": seq},
        {"branch": branch, "seq": across},
        {"branch": near, "seq": seq},
        {"branch": near, "seq": across},
    ]
    holders = [(p["branch"] * n_seq + p["seq"]) // 2 for p in places]

    def remote(src, dst, send, arrive, device):
        return pltpu.make_async_remote_copy(
            src_ref=src, dst_ref=dst, send_sem=send, recv_sem=arrive,
            device_id=device, device_id_type=mesh_id,
        )

    def part(c):
        return slice(c * step, (c + 1) * step)

    twin = {"seq": seq + 1 - 2 * (seq % 2)}
    weights = []
    for i, (src, dst) in enumerate(((wgu_ref, wgu), (wdn_ref, wdn))):
        weights.append(pltpu.make_async_copy(src, dst.at[0], wloc.at[i]))
        weights.append(remote(src, dst.at[1], wsend.at[i], wrecv.at[i], twin))
    mine = pltpu.make_async_copy(kv_ref, own.at[0], kloc)
    mine.start()

    barrier = pltpu.get_barrier_semaphore()
    for shift in range(1, n_branch):
        pl.semaphore_signal(
            barrier, inc=1, device_id={"branch": (branch + shift) % n_branch}, device_id_type=mesh_id
        )
    for shift in range(1, n_seq):
        pl.semaphore_signal(
            barrier, inc=1, device_id={"seq": (seq + shift) % n_seq}, device_id_type=mesh_id
        )
    pl.semaphore_wait(barrier, n_branch + n_seq - 2)

    def share(shift):
        return remote(
            kv_ref, own.at[shift], ksend.at[shift - 1], krecv.at[shift - 1],
            {"seq": (seq + shift) % n_seq},
        )

    for shift in range(1, n_seq):
        share(shift).start()
    for copy in weights:
        copy.start()

    idt = idt_ref[...]
    top_count = idt.shape[0]
    kinds_t = lax.broadcasted_iota(jnp.int32, (experts, rows), 0)
    hot_t = [(idt[k : k + 1, :] == kinds_t).astype(F32) for k in range(top_count)]
    down = lax.broadcasted_iota(jnp.int32, (rows, rows), 0)
    along = lax.broadcasted_iota(jnp.int32, (rows, rows), 1)
    before_t = jnp.dot(
        sum(hot_t).astype(BF16), (down < along).astype(F32).astype(BF16), preferred_element_type=F32
    )
    meta[...] = jnp.zeros_like(meta)
    for k in range(top_count):
        slot_t = jnp.sum(before_t * hot_t[k], axis=0, keepdims=True)
        meta[k : k + 1, :] = idt[k : k + 1, :].astype(F32) * float(cap) + slot_t

    mine.wait()
    for shift in range(1, n_seq):
        share(shift).wait_recv()
    for offset in range(n_branch - 1):
        picked[offset] = own[(seq - list_ref[offset] + n_seq) % n_seq]

    def lend(offset):
        return remote(
            picked.at[offset], sib.at[offset], ssend.at[offset], srecv.at[offset],
            {"branch": (branch + offset + 1) % n_branch},
        )

    for offset in range(n_branch - 1):
        lend(offset).start()

    def chunk(r):
        return pl.ds(pl.multiple_of(r * span, span), span)

    def columns(head, half):
        base = (head * group + half * pack) * HEAD_SIZE
        return [slice(base + i * HEAD_SIZE, base + (i + 1) * HEAD_SIZE) for i in range(pack)]

    def kv_cols(head):
        return (
            slice(head * HEAD_SIZE, (head + 1) * HEAD_SIZE),
            slice((kv_heads + head) * HEAD_SIZE, (kv_heads + head + 1) * HEAD_SIZE),
        )

    tall = pack * span

    @pl.loop(0, CHUNKS)
    def _(r):
        at_row = r * span + lax.broadcasted_iota(jnp.int32, (tall, own_len), 0) % span
        at_col = lax.broadcasted_iota(jnp.int32, (tall, own_len), 1)
        earlier = at_col // rows
        bias = jnp.where(
            earlier == 0,
            jnp.where(at_col <= at_row, 0.0, -1e30),
            jnp.where(earlier <= seq, 0.0, -1e30),
        )
        for head in range(kv_heads):
            kcol, vcol = kv_cols(head)
            for half in range(halves):
                cols = columns(head, half)
                q = jnp.concatenate([q_ref[chunk(r), c] for c in cols], axis=0)
                keys = own[:, :, kcol].reshape(own_len, HEAD_SIZE)
                values = own[:, :, vcol].reshape(own_len, HEAD_SIZE)
                scores = lax.dot_general(q, keys, nt, preferred_element_type=F32) * scale + bias
                top = jnp.max(scores, axis=1, keepdims=True)
                p = jnp.exp(scores - top)
                tops[r, head * halves + half] = top
                totals[r, head * halves + half] = jnp.sum(p, axis=1, keepdims=True)
                mixed = jnp.dot(p.astype(BF16), values, preferred_element_type=F32)
                for i, c in enumerate(cols):
                    state[chunk(r), c] = mixed[i * span : (i + 1) * span]

    for offset in range(n_branch - 1):
        lend(offset).wait_recv()

    def rows_out(r):
        return remote(
            norm.at[chunk(r)], raw.at[inner, chunk(r)], rowsend.at[r], rowrecv.at[inner, r],
            {"branch": onward},
        )

    @pl.loop(0, CHUNKS)
    def _(r):
        for head in range(kv_heads):
            kcol, vcol = kv_cols(head)
            for half in range(halves):
                cols = columns(head, half)
                q = jnp.concatenate([q_ref[chunk(r), c] for c in cols], axis=0)
                keys = sib[:, :, kcol].reshape(sib_len, HEAD_SIZE)
                values = sib[:, :, vcol].reshape(sib_len, HEAD_SIZE)
                scores = lax.dot_general(q, keys, nt, preferred_element_type=F32) * scale
                own_top = tops[r, head * halves + half]
                top = jnp.maximum(own_top, jnp.max(scores, axis=1, keepdims=True))
                p = jnp.exp(scores - top)
                shrink = jnp.exp(own_top - top)
                total = totals[r, head * halves + half] * shrink + jnp.sum(p, axis=1, keepdims=True)
                mixed = jnp.dot(p.astype(BF16), values, preferred_element_type=F32)
                inverse = 1.0 / total
                for i, c in enumerate(cols):
                    at = slice(i * span, (i + 1) * span)
                    context = (state[chunk(r), c] * shrink[at] + mixed[at]) * inverse[at]
                    state[chunk(r), c] = res_ref[chunk(r), c].astype(F32) + context.astype(BF16).astype(F32)
        full = state[chunk(r), :]
        norm[chunk(r), :] = (
            full * lax.rsqrt(jnp.mean(full * full, axis=1, keepdims=True) + 1e-06)
        ).astype(BF16)
        rows_out(r).start()

    logits_t = lax.dot_general(router_ref[...], norm[...], nt, preferred_element_type=F32)
    chosen_t = [jnp.sum(logits_t * hot_t[k], axis=0, keepdims=True) for k in range(top_count)]
    for k in range(top_count):
        meta[top_count + k : top_count + k + 1, :] = 1.0 / sum(
            jnp.exp(c - chosen_t[k]) for c in chosen_t
        )

    def meta_out():
        return remote(meta, xmeta.at[inner], msend.at[0], mrecv.at[inner], {"branch": onward})

    meta_out().start()

    def relay(c):
        return remote(
            raw.at[0, :, part(c)], raw.at[2, :, part(c)], relsend.at[c], relrecv.at[c], {"branch": far}
        )

    def meta_relay():
        return remote(xmeta.at[0], xmeta.at[2], msend.at[1], mrecv.at[2], {"branch": far})

    def meta_of(g):
        return meta[...] if g == 0 else xmeta[g - 1]

    def slots_of(g, count):
        where = lax.broadcasted_iota(jnp.int32, (cap, rows), 0).astype(F32)
        given = meta_of(g)
        return given, [where + (holders[f] * cap).astype(F32) for f in range(count)]

    def picks(g, count):
        given, where = slots_of(g, count)
        return jnp.concatenate(
            [(given[0:1] == w).astype(F32) + (given[1:2] == w).astype(F32) for w in where], axis=0
        ).astype(BF16)

    def shares(g, count):
        given, where = slots_of(g, count)
        weight = jnp.concatenate(
            [
                jnp.where(given[0:1] == w, given[2:3], 0.0) + jnp.where(given[1:2] == w, given[3:4], 0.0)
                for w in where
            ],
            axis=0,
        ).T
        high = weight.astype(BF16)
        return high, (weight - high.astype(F32)).astype(BF16)

    def spot(g, f):
        if f == 1:
            return g, 1
        return (1 if g == 0 else g), f - 2

    def forward(g, f, c):
        tg, th = spot(g, f)
        return remote(
            fwd.at[g, f - 1, :, part(c)], recv.at[tg, th, :, part(c)],
            fsend.at[g, f - 1], drecv.at[tg, th], places[f],
        )

    def give(g, count, pick, c):
        source = norm[:, part(c)] if g == 0 else raw[g - 1, :, part(c)]
        taken = jnp.dot(pick, source, preferred_element_type=F32).astype(BF16)
        recv[g, 0, :, part(c)] = taken[:cap]
        for f in range(1, count):
            fwd[g, f - 1, :, part(c)] = taken[f * cap : (f + 1) * cap]
        for f in ((3, 2, 1) if count == 4 else (1,)):
            forward(g, f, c).start()

    def give_all(g, count):
        pick = picks(g, count)
        for c in range(PARTS):
            give(g, count, pick, c)

    def whole(g, h):
        return remote(recv.at[g, h], recv.at[g, h], fsend.at[0, 0], drecv.at[g, h], places[1])

    def home(g, f, c):
        if f == 1:
            return g, 0
        return (0 if g == 1 else g), f - 1

    def hand(g, f, c):
        tg, slot = home(g, f, c)
        h = 1 if f == 1 else f - 2
        return remote(
            res.at[g, h, :, part(c)], back.at[tg, slot, :, part(c)],
            bsend.at[g, h], brecv.at[tg, slot, c], places[f],
        )

    def compute(g):
        whole(g, 1).wait_recv()
        if g:
            pl.when(inner == 0)(lambda: whole(g, 0).wait_recv())
        x = recv[g].reshape(2 * cap, width)
        acts = []
        for h in range(2):
            gate = jnp.dot(x, wgu[h, 0], preferred_element_type=F32)
            up = jnp.dot(x, wgu[h, 1], preferred_element_type=F32)
            acts.append((gate / (1.0 + jnp.exp(-gate)) * up).astype(BF16))
        for c in range(PARTS):
            done = jnp.dot(acts[0], wdn[0, :, part(c)], preferred_element_type=F32)
            done += jnp.dot(acts[1], wdn[1, :, part(c)], preferred_element_type=F32)
            res[g, :, :, part(c)] = done.astype(BF16).reshape(2, cap, step)
            if g == 0:
                hand(0, 1, c).start()
            else:

                def side():
                    hand(g, 1, c).start()

                def up_line():
                    hand(g, 3, c).start()
                    hand(g, 2, c).start()

                pl.when(inner == 1)(side)
                pl.when(inner == 0)(up_line)

    def combined(g, count, weight, c):
        for f in range(count - 1):
            remote(
                back.at[g, f, :, part(c)], back.at[g, f, :, part(c)],
                bsend.at[0, 0], brecv.at[g, f, c], places[1],
            ).wait_recv()
        given = jnp.concatenate(
            [res[g, 0, :, part(c)]] + [back[g, f, :, part(c)] for f in range(count - 1)], axis=0
        )
        return jnp.dot(weight[0], given, preferred_element_type=F32) + jnp.dot(
            weight[1], given, preferred_element_type=F32
        )

    def result(s, c):
        if s == 2:
            return remote(xout.at[2, c], fin.at[0, c], osend.at[2, c], orecv.at[0, c], {"branch": near})
        return remote(xout.at[s, c], fin.at[s, c], osend.at[s, c], orecv.at[s, c], {"branch": far})

    def wait_rows(g):
        remote(xmeta.at[g - 1], xmeta.at[g - 1], msend.at[0], mrecv.at[g - 1], places[2]).wait_recv()
        if g < 3:
            for r in range(CHUNKS):
                at = slice(r * span, (r + 1) * span)
                remote(
                    raw.at[g - 1, at], raw.at[g - 1, at], rowsend.at[0], rowrecv.at[g - 1, r], places[2]
                ).wait_recv()

    is_inner = pl.when(inner == 1)
    is_outer = pl.when(inner == 0)

    is_inner(lambda: give_all(0, 4))
    is_outer(lambda: give_all(0, 2))

    for copy in weights:
        copy.wait()
    compute(0)

    @is_inner
    def _():
        wait_rows(1)
        for c in range(PARTS):
            relay(c).start()
        meta_relay().start()
        wait_rows(2)
        give_all(2, 4)
        give_all(1, 2)

    compute(1)

    def far_rows(c):
        relay_in = remote(
            raw.at[2, :, part(c)], raw.at[2, :, part(c)], relsend.at[0], relrecv.at[c], places[2]
        )
        relay_in.wait_recv()

    @is_inner
    def _():
        wait_rows(3)
        pick = picks(3, 4)
        for c in range(PARTS):
            far_rows(c)
            give(3, 4, pick, c)

    compute(2)
    compute(3)

    @is_inner
    def _():
        for s in range(2):
            weight = shares(2 + s, 4)
            for c in range(PARTS):
                xout[s, c] = combined(2 + s, 4, weight, c).astype(BF16)
                result(s, c).start()
        weight = shares(0, 4)
        for c in range(PARTS):
            state[:, part(c)] += combined(0, 4, weight, c)

    @is_outer
    def _():
        weight = shares(0, 2)
        for c in range(PARTS):
            state[:, part(c)] += combined(0, 2, weight, c)

    def arrived(s, c):
        remote(fin.at[s, c], fin.at[s, c], osend.at[0, 0], orecv.at[s, c], places[2]).wait_recv()

    for c in range(PARTS):
        arrived(0, c)
        out_ref[:, part(c)] = (state[:, part(c)] + fin[0, c].astype(F32)).astype(BF16)

    @is_inner
    def _():
        weight = shares(1, 2)
        for c in range(PARTS):
            partial = combined(1, 2, weight, c)
            arrived(1, c)
            xout[2, c] = (partial + fin[1, c].astype(F32)).astype(BF16)
            result(2, c).start()

    for shift in range(1, n_seq):
        share(shift).wait_send()
    for offset in range(n_branch - 1):
        lend(offset).wait_send()
    for r in range(CHUNKS):
        rows_out(r).wait_send()
    meta_out().wait_send()

    def sent(g, f):
        remote(fwd.at[g, f - 1], fwd.at[g, f - 1], fsend.at[g, f - 1], drecv.at[0, 0], places[1]).wait_send()

    def returned(g, h):
        remote(res.at[g, h], res.at[g, h], bsend.at[g, h], brecv.at[0, 0, 0], places[1]).wait_send()

    sent(0, 1)
    returned(0, 1)

    @is_inner
    def _():
        for g in (0, 2, 3):
            for f in ((2, 3) if g == 0 else (1, 2, 3)):
                sent(g, f)
        sent(1, 1)
        for g in (1, 2, 3):
            returned(g, 1)
        for c in range(PARTS):
            relay(c).wait_send()
            for s in range(3):
                result(s, c).wait_send()
        meta_relay().wait_send()

    @is_outer
    def _():
        for g in (1, 2, 3):
            for h in range(2):
                returned(g, h)


def run_line(listed, q, kv, residual, router_t, idt, wgu, wdn, experts, cap, n_branch, n_seq):
    rows, width = q.shape
    ff = wdn.shape[0]
    part = width // PARTS
    tall = 2 * rows
    steps = width // HEAD_SIZE * rows // tall // CHUNKS
    dma = pltpu.SemaphoreType.DMA
    return pl.pallas_call(
        functools.partial(line_kernel, experts, cap, n_branch, n_seq),
        out_shape=jax.ShapeDtypeStruct((rows, width), BF16),
        in_specs=[SMEM] + [VMEM] * 5 + [ANY, ANY],
        out_specs=VMEM,
        scratch_shapes=[
            pltpu.VMEM((n_seq, rows, kv.shape[1]), BF16),
            pltpu.VMEM((n_branch - 1, rows, kv.shape[1]), BF16),
            pltpu.VMEM((n_branch - 1, rows, kv.shape[1]), BF16),
            pltpu.VMEM((CHUNKS, steps, tall, 1), F32),
            pltpu.VMEM((CHUNKS, steps, tall, 1), F32),
            pltpu.VMEM((rows, width), F32),
            pltpu.VMEM((rows, width), BF16),
            pltpu.VMEM((3, rows, width), BF16),
            pltpu.VMEM((8, rows), F32),
            pltpu.VMEM((3, 8, rows), F32),
            pltpu.VMEM((4, 2, cap, width), BF16),
            pltpu.VMEM((4, 2, cap, width), BF16),
            pltpu.VMEM((4, 3, cap, width), BF16),
            pltpu.VMEM((4, 3, cap, width), BF16),
            pltpu.VMEM((2, 2, width, ff), BF16),
            pltpu.VMEM((2, ff, width), BF16),
            pltpu.VMEM((3, PARTS, rows, part), BF16),
            pltpu.VMEM((2, PARTS, rows, part), BF16),
            dma, dma((n_seq - 1,)), dma((n_seq - 1,)), dma((n_branch - 1,)), dma((n_branch - 1,)),
            dma((2,)), dma((2,)), dma((2,)),
            dma((CHUNKS,)), dma((2, CHUNKS)), dma((PARTS,)), dma((PARTS,)), dma((2,)), dma((3,)),
            dma((4, 3)), dma((4, 2)), dma((4, 2)), dma((4, 3, PARTS)), dma((3, PARTS)), dma((2, PARTS)),
        ],
        compiler_params=pltpu.CompilerParams(
            collective_id=2, has_side_effects=True, vmem_limit_bytes=VMEM_LIMIT
        ),
    )(listed, q, kv, residual, router_t, idt, wgu, wdn)


def on_device(
    n_branch, n_seq, queries, keyvals, residual, read_list, router, expert_ids, w_gate_up, w_down
):
    rows = queries.shape[1]
    experts = router.shape[1]
    top_count = expert_ids.shape[2]
    capacity = 2 * ((3 * rows * top_count + 4 * experts - 1) // (4 * experts))
    cap = (capacity + 15) // 16 * 16
    kv = keyvals.reshape(rows, -1)
    wgu = jnp.swapaxes(w_gate_up[0], 0, 1)
    if n_branch == 4 and n_seq == 4 and experts == 8 and top_count == 2:
        return run_line(
            read_list.reshape(-1), queries[0], kv, residual[0], router.T, expert_ids[0].T,
            wgu, w_down[0], experts, cap, n_branch, n_seq,
        )[None]
    shifts = [
        lax.ppermute(kv, "seq", [(i, (i + step) % n_seq) for i in range(n_seq)])
        for step in range(1, n_seq)
    ]
    own = jnp.stack([kv] + shifts)
    send, state, gate, normed, meta = attend(
        read_list.reshape(-1), queries[0], own, residual[0], router.T, expert_ids[0],
        experts, experts, cap, n_branch, n_seq,
    )
    return run_experts(send, state, gate, wgu, w_down[0], experts, cap, n_seq)[None]


def solution(mesh):
    return jax.shard_map(
        functools.partial(on_device, mesh.shape["branch"], mesh.shape["seq"]),
        mesh=mesh,
        in_specs=(
            P(("rollout", "branch"), "seq", None),
            P(("rollout", "branch"), "seq", None, None),
            P(("rollout", "branch"), "seq", None),
            P(("rollout", "branch"), "seq", None),
            P(),
            P(("rollout", "branch"), "seq", None),
            P(("branch", "seq"), None, None, None),
            P(("branch", "seq"), None, None),
        ),
        out_specs=P(("rollout", "branch"), "seq", None),
        check_vma=False,
    )
```

```python
import functools
import math

import jax
import jax.numpy as jnp
from jax import lax
from jax.experimental import pallas as pl
from jax.experimental.pallas import tpu as pltpu
from jax.sharding import PartitionSpec as P

HEAD_SIZE = 128
PARTS = 8
CHUNKS = 4
SLABS = 4
VMEM_LIMIT = 60 * 1024 * 1024
LINE_VMEM_LIMIT = 63 * 1024 * 1024
F32 = jnp.float32
BF16 = jnp.bfloat16
ANY = pl.BlockSpec(memory_space=pl.ANY)
VMEM = pl.BlockSpec(memory_space=pltpu.VMEM)
SMEM = pl.BlockSpec(memory_space=pltpu.SMEM)


def flipped(number, mask, count):
    value, bit = 0, 1
    while bit < count:
        value = value + ((number // bit + mask // bit) % 2) * bit
        bit *= 2
    return value


def attend_kernel(
    experts, cap, n_branch, n_seq,
    list_ref, q_ref, own_ref, res_ref, router_ref, ids_ref, idt_ref,
    send_ref, state_ref, gate_ref, norm_ref, meta_ref,
    picked, sib_ref, tops, totals, ssem, rsem,
):
    branch = lax.axis_index("branch")
    seq = lax.axis_index("seq")
    me = (branch * n_seq + seq) // 2
    rows, width = q_ref.shape
    kv_heads = own_ref.shape[2] // (2 * HEAD_SIZE)
    group = width // HEAD_SIZE // kv_heads
    together = 2
    tall = together * rows
    own_len = n_seq * rows
    sib_len = (n_branch - 1) * rows
    scale = 1.0 / math.sqrt(HEAD_SIZE)
    nt = (((1,), (1,)), ((), ()))

    barrier = pltpu.get_barrier_semaphore()
    for step in range(1, n_branch):
        pl.semaphore_signal(
            barrier, inc=1, device_id={"branch": (branch + step) % n_branch},
            device_id_type=pl.DeviceIdType.MESH,
        )
    for offset in range(n_branch - 1):
        picked[offset] = own_ref[(seq - list_ref[offset] + n_seq) % n_seq]
    pl.semaphore_wait(barrier, n_branch - 1)
    copies = []
    for offset in range(n_branch - 1):
        copy = pltpu.make_async_remote_copy(
            src_ref=picked.at[offset], dst_ref=sib_ref.at[offset],
            send_sem=ssem.at[offset], recv_sem=rsem.at[offset],
            device_id={"branch": (branch + offset + 1) % n_branch},
            device_id_type=pl.DeviceIdType.MESH,
        )
        copy.start()
        copies.append(copy)

    at_row = lax.broadcasted_iota(jnp.int32, (tall, own_len), 0) % rows
    at_col = lax.broadcasted_iota(jnp.int32, (tall, own_len), 1)
    earlier = at_col // rows
    bias = jnp.where(
        earlier == 0,
        jnp.where(at_col <= at_row, 0.0, -1e30),
        jnp.where(earlier <= seq, 0.0, -1e30),
    )

    def head_parts(head, step):
        base = (head * group + step * together) * HEAD_SIZE
        cols = [
            pl.ds(pl.multiple_of(base + i * HEAD_SIZE, HEAD_SIZE), HEAD_SIZE)
            for i in range(together)
        ]
        return cols, jnp.concatenate([q_ref[:, c] for c in cols], axis=0)

    def kv_cols(head):
        return (
            slice(head * HEAD_SIZE, (head + 1) * HEAD_SIZE),
            slice((kv_heads + head) * HEAD_SIZE, (kv_heads + head + 1) * HEAD_SIZE),
        )

    steps = group // together
    for head in range(kv_heads):
        kcol, vcol = kv_cols(head)

        @pl.loop(0, steps)
        def _(step):
            cols, q = head_parts(head, step)
            keys = own_ref[:, :, kcol].reshape(own_len, HEAD_SIZE)
            values = own_ref[:, :, vcol].reshape(own_len, HEAD_SIZE)
            scores = lax.dot_general(q, keys, nt, preferred_element_type=F32) * scale + bias
            top = jnp.max(scores, axis=1, keepdims=True)
            p = jnp.exp(scores - top)
            tops[head * steps + step] = top
            totals[head * steps + step] = jnp.sum(p, axis=1, keepdims=True)
            mixed = jnp.dot(p.astype(BF16), values, preferred_element_type=F32)
            for i, c in enumerate(cols):
                state_ref[:, c] = mixed[i * rows : (i + 1) * rows]

    for copy in copies:
        copy.wait()
    for head in range(kv_heads):
        kcol, vcol = kv_cols(head)

        @pl.loop(0, steps)
        def _(step):
            cols, q = head_parts(head, step)
            keys = sib_ref[:, :, kcol].reshape(sib_len, HEAD_SIZE)
            values = sib_ref[:, :, vcol].reshape(sib_len, HEAD_SIZE)
            scores = lax.dot_general(q, keys, nt, preferred_element_type=F32) * scale
            own_top = tops[head * steps + step]
            top = jnp.maximum(own_top, jnp.max(scores, axis=1, keepdims=True))
            p = jnp.exp(scores - top)
            shrink = jnp.exp(own_top - top)
            total = totals[head * steps + step] * shrink + jnp.sum(p, axis=1, keepdims=True)
            mixed = jnp.dot(p.astype(BF16), values, preferred_element_type=F32)
            inverse = 1.0 / total
            for i, c in enumerate(cols):
                part = slice(i * rows, (i + 1) * rows)
                context = (state_ref[:, c] * shrink[part] + mixed[part]) * inverse[part]
                state_ref[:, c] = res_ref[:, c].astype(F32) + context.astype(BF16).astype(F32)

    state = state_ref[...]
    normed = (
        state * lax.rsqrt(jnp.mean(state * state, axis=1, keepdims=True) + 1e-06)
    ).astype(BF16)
    logits = lax.dot_general(normed, router_ref[...], nt, preferred_element_type=F32)

    top_count = ids_ref.shape[1]
    ids, idt = ids_ref[...], idt_ref[...]
    kinds = lax.broadcasted_iota(jnp.int32, (rows, experts), 1)
    kinds_t = lax.broadcasted_iota(jnp.int32, (experts, rows), 0)
    hot = [(ids[:, k : k + 1] == kinds).astype(F32) for k in range(top_count)]
    hot_t = [(idt[k : k + 1, :] == kinds_t).astype(F32) for k in range(top_count)]
    down = lax.broadcasted_iota(jnp.int32, (rows, rows), 0)
    along = lax.broadcasted_iota(jnp.int32, (rows, rows), 1)
    before = jnp.dot((along < down).astype(F32).astype(BF16), sum(hot).astype(BF16), preferred_element_type=F32)
    before_t = jnp.dot(sum(hot_t).astype(BF16), (down < along).astype(F32).astype(BF16), preferred_element_type=F32)
    dest, dest_t = [], []
    for k in range(top_count):
        slot = jnp.sum(before * hot[k], axis=1, keepdims=True).astype(jnp.int32)
        dest.append((ids[:, k : k + 1] ^ me) * cap + slot)
        slot_t = jnp.sum(before_t * hot_t[k], axis=0, keepdims=True).astype(jnp.int32)
        dest_t.append((idt[k : k + 1, :] ^ me) * cap + slot_t)
    chosen = [jnp.sum(logits * hot[k], axis=1, keepdims=True) for k in range(top_count)]
    gates = [1.0 / sum(jnp.exp(c - chosen[k]) for c in chosen) for k in range(top_count)]

    parts, _, part_width = norm_ref.shape
    for c in range(parts):
        norm_ref[c] = normed[:, c * part_width : (c + 1) * part_width]
    logits_t = lax.dot_general(router_ref[...], normed, nt, preferred_element_type=F32)
    chosen_t = [jnp.sum(logits_t * hot_t[k], axis=0, keepdims=True) for k in range(top_count)]
    meta_ref[...] = jnp.zeros_like(meta_ref)
    for k in range(top_count):
        meta_ref[k : k + 1, :] = dest_t[k].astype(F32)
        meta_ref[top_count + k : top_count + k + 1, :] = 1.0 / sum(
            jnp.exp(c - chosen_t[k]) for c in chosen_t
        )

    pair = 2 * cap
    places = lax.broadcasted_iota(jnp.int32, (rows, pair), 1)
    places_t = lax.broadcasted_iota(jnp.int32, (pair, rows), 0)
    for p in range(send_ref.shape[0] // pair):
        pick = sum((dest_t[k] - p * pair == places_t).astype(F32) for k in range(top_count))
        send_ref[p * pair : (p + 1) * pair, :] = jnp.dot(
            pick.astype(BF16), normed, preferred_element_type=F32
        ).astype(BF16)
        weight = sum(
            jnp.where(dest[k] - p * pair == places, gates[k], 0.0) for k in range(top_count)
        )
        high = weight.astype(BF16)
        gate_ref[p, 0] = high
        gate_ref[p, 1] = (weight - high.astype(F32)).astype(BF16)


def attend(listed, q, own, residual, router_t, ids, experts, near, cap, n_branch, n_seq):
    rows, width = q.shape
    halves = width // HEAD_SIZE // 2
    return pl.pallas_call(
        functools.partial(attend_kernel, experts, cap, n_branch, n_seq),
        out_shape=(
            jax.ShapeDtypeStruct((near * cap, width), BF16),
            jax.ShapeDtypeStruct((rows, width), F32),
            jax.ShapeDtypeStruct((near // 2, 2, rows, 2 * cap), BF16),
            jax.ShapeDtypeStruct((PARTS, rows, width // PARTS), BF16),
            jax.ShapeDtypeStruct((8, rows), F32),
        ),
        in_specs=[SMEM] + [VMEM] * 6,
        out_specs=(VMEM,) * 5,
        scratch_shapes=[
            pltpu.VMEM((n_branch - 1, rows, own.shape[2]), BF16),
            pltpu.VMEM((n_branch - 1, rows, own.shape[2]), BF16),
            pltpu.VMEM((halves, 2 * rows, 1), F32),
            pltpu.VMEM((halves, 2 * rows, 1), F32),
            pltpu.SemaphoreType.DMA((n_branch,)),
            pltpu.SemaphoreType.DMA((n_branch,)),
        ],
        compiler_params=pltpu.CompilerParams(
            collective_id=0, has_side_effects=True, vmem_limit_bytes=VMEM_LIMIT
        ),
    )(listed, q, own, residual, router_t, ids, ids.T)


def expert_kernel(
    experts, cap, n_seq,
    send_ref, state_ref, gate_ref, wgu_ref, wdn_ref, out_ref,
    recv, res, ret, wgu, wdn, acc,
    wsend, wrecv, wloc, lsem, dsend, drecv, bsend, brecv,
):
    branch = lax.axis_index("branch")
    seq = lax.axis_index("seq")
    core = seq % 2
    me = (branch * n_seq + seq) // 2
    pair = 2 * cap
    width = send_ref.shape[1]
    twin = {"seq": seq + 1 - 2 * core}
    mesh_id = pl.DeviceIdType.MESH

    def place(k):
        other = flipped(me, k, experts)
        return {"branch": (2 * other) // n_seq, "seq": (2 * other) % n_seq + core}

    barrier = pltpu.get_barrier_semaphore()
    pl.semaphore_signal(barrier, inc=1, device_id=twin, device_id_type=mesh_id)

    @pl.loop(1, experts)
    def _(k):
        pl.semaphore_signal(barrier, inc=1, device_id=place(k), device_id_type=mesh_id)

    pl.semaphore_wait(barrier, experts)

    def block(k):
        return pl.ds(pl.multiple_of(k * cap, 16), cap)

    def dispatch(k):
        return pltpu.make_async_remote_copy(
            src_ref=send_ref.at[block(k)], dst_ref=recv.at[block(k)],
            send_sem=dsend.at[k], recv_sem=drecv.at[k],
            device_id=place(k), device_id_type=mesh_id,
        )

    def give_back(k):
        return pltpu.make_async_remote_copy(
            src_ref=res.at[block(k)], dst_ref=ret.at[block(k)],
            send_sem=bsend.at[k], recv_sem=brecv.at[k],
            device_id=place(k), device_id_type=mesh_id,
        )

    weights = []
    for i, (src, dst) in enumerate(((wgu_ref, wgu), (wdn_ref, wdn))):
        weights.append(
            pltpu.make_async_remote_copy(
                src_ref=src, dst_ref=dst.at[1], send_sem=wsend.at[i], recv_sem=wrecv.at[i],
                device_id=twin, device_id_type=mesh_id,
            )
        )
        weights.append(pltpu.make_async_copy(src, dst.at[0], wloc.at[i]))
    dispatch(1).start()
    mine = pltpu.make_async_copy(send_ref.at[block(0)], recv.at[block(0)], lsem)
    mine.start()

    @pl.loop(experts // 2, experts)
    def _(k):
        dispatch(k).start()

    @pl.loop(2, experts // 2)
    def _(k):
        dispatch(k).start()

    for copy in weights:
        copy.start()
    acc[...] = state_ref[...]
    for copy in weights:
        copy.wait()

    chunk = 512

    def compute(p):
        span = pl.ds(pl.multiple_of(p * pair, 16), pair)
        acts = []
        for h in range(2):
            x = recv[span, :]
            gate = jnp.dot(x, wgu[h, 0], preferred_element_type=F32)
            up = jnp.dot(x, wgu[h, 1], preferred_element_type=F32)
            acts.append((gate / (1.0 + jnp.exp(-gate)) * up).astype(BF16))
        for start in range(0, width, chunk):
            cols = slice(start, start + chunk)
            done = jnp.dot(acts[0], wdn[0, :, cols], preferred_element_type=F32)
            done += jnp.dot(acts[1], wdn[1, :, cols], preferred_element_type=F32)
            res[span, cols] = done.astype(BF16)

    quarter = experts // 4

    def turn(i):
        return jnp.where(i <= quarter, i + quarter - 1, i - quarter)

    mine.wait()
    dispatch(1).wait_recv()
    compute(0)
    give_back(1).start()

    @pl.loop(1, experts // 2)
    def _(i):
        p = turn(i)
        dispatch(2 * p).wait_recv()
        dispatch(2 * p + 1).wait_recv()
        compute(p)
        give_back(2 * p).start()
        give_back(2 * p + 1).start()

    def add(p, rows):
        for start in range(0, width, chunk):
            cols = slice(start, start + chunk)
            block_rows = rows(cols)
            acc[:, cols] += jnp.dot(
                gate_ref[p, 0], block_rows, preferred_element_type=F32
            ) + jnp.dot(gate_ref[p, 1], block_rows, preferred_element_type=F32)

    give_back(1).wait_recv()
    add(0, lambda cols: jnp.concatenate([res[0:cap, cols], ret[cap:pair, cols]], axis=0))

    @pl.loop(1, experts // 2)
    def _(i):
        p = turn(i)
        give_back(2 * p).wait_recv()
        give_back(2 * p + 1).wait_recv()
        span = pl.ds(pl.multiple_of(p * pair, 16), pair)
        add(p, lambda cols: ret[span, cols])

    out_ref[...] = acc[...].astype(BF16)

    @pl.loop(1, experts)
    def _(k):
        dispatch(k).wait_send()
        give_back(k).wait_send()


def run_experts(send, state, gate, wgu, wdn, experts, cap, n_seq):
    rows, width = state.shape
    ff = wdn.shape[0]
    return pl.pallas_call(
        functools.partial(expert_kernel, experts, cap, n_seq),
        out_shape=jax.ShapeDtypeStruct((rows, width), BF16),
        in_specs=[ANY, VMEM, VMEM, ANY, ANY],
        out_specs=VMEM,
        scratch_shapes=[
            pltpu.VMEM((experts * cap, width), BF16),
            pltpu.VMEM((experts * cap, width), BF16),
            pltpu.VMEM((experts * cap, width), BF16),
            pltpu.VMEM((2, 2, width, ff), BF16),
            pltpu.VMEM((2, ff, width), BF16),
            pltpu.VMEM((rows, width), F32),
            pltpu.SemaphoreType.DMA((2,)),
            pltpu.SemaphoreType.DMA((2,)),
            pltpu.SemaphoreType.DMA((2,)),
            pltpu.SemaphoreType.DMA,
            pltpu.SemaphoreType.DMA((experts,)),
            pltpu.SemaphoreType.DMA((experts,)),
            pltpu.SemaphoreType.DMA((experts,)),
            pltpu.SemaphoreType.DMA((experts,)),
        ],
        compiler_params=pltpu.CompilerParams(
            collective_id=1, has_side_effects=True, vmem_limit_bytes=VMEM_LIMIT
        ),
    )(send, state, gate, wgu, wdn)


def line_kernel(
    experts, cap, n_branch, n_seq,
    list_ref, q_ref, kv_ref, res_ref, router_ref, idt_ref, wgu_ref, wdn_ref,
    out_ref,
    own, picked, sib, tops, totals, state, norm, raw, meta, xmeta,
    recv, res, back, fwd, wraw, wgu, wdn, xout, fin,
    ksend, krecv, ssend, srecv, wsend, wrecv, wloc,
    rowsend, rowrecv, relsend, relrecv, msend, mrecv,
    fsend, drecv, bsend, brecv, lsend, osend, orecv,
):
    branch = lax.axis_index("branch")
    seq = lax.axis_index("seq")
    inner = (branch + 1) // 2 % 2
    mesh_id = pl.DeviceIdType.MESH
    rows, width = q_ref.shape
    kv_heads = own.shape[2] // (2 * HEAD_SIZE)
    group = width // HEAD_SIZE // kv_heads
    own_len = n_seq * rows
    sib_len = (n_branch - 1) * rows
    scale = 1.0 / math.sqrt(HEAD_SIZE)
    nt = (((1,), (1,)), ((), ()))
    step = width // PARTS
    span = rows // CHUNKS
    pack = 2 * rows // span
    halves = group // pack

    across = (seq + 2) % n_seq
    near = branch + 1 - 2 * (branch % 2)
    far = n_branch - 1 - branch
    onward = near + inner * (far - near)
    places = [
        {"branch": branch, "seq": seq},
        {"branch": branch, "seq": across},
        {"branch": near, "seq": seq},
        {"branch": near, "seq": across},
    ]
    holders = [(p["branch"] * n_seq + p["seq"]) // 2 for p in places]

    def remote(src, dst, send, arrive, device):
        return pltpu.make_async_remote_copy(
            src_ref=src, dst_ref=dst, send_sem=send, recv_sem=arrive,
            device_id=device, device_id_type=mesh_id,
        )

    def part(c):
        return slice(c * step, (c + 1) * step)

    twin = {"seq": seq + 1 - 2 * (seq % 2)}
    slab = width // SLABS

    def slab_in(i):
        at = slice(i * slab, (i + 1) * slab)
        return pltpu.make_async_copy(wgu_ref.at[at], wraw.at[at], wloc.at[i])

    def slab_out(i):
        at = slice(i * slab, (i + 1) * slab)
        return remote(wgu.at[0, :, at], wgu.at[1, :, at], wsend.at[i], wrecv.at[i], twin)

    down_in = pltpu.make_async_copy(wdn_ref, wdn.at[0], wloc.at[SLABS])
    down_out = remote(wdn_ref, wdn.at[1], wsend.at[SLABS], wrecv.at[SLABS], twin)
    for i in range(SLABS):
        slab_in(i).start()
    down_in.start()
    own[0] = kv_ref[...].reshape(rows, own.shape[2])

    barrier = pltpu.get_barrier_semaphore()
    for shift in range(1, n_branch):
        pl.semaphore_signal(
            barrier, inc=1, device_id={"branch": (branch + shift) % n_branch}, device_id_type=mesh_id
        )
    for shift in range(1, n_seq):
        pl.semaphore_signal(
            barrier, inc=1, device_id={"seq": (seq + shift) % n_seq}, device_id_type=mesh_id
        )
    pl.semaphore_wait(barrier, n_branch + n_seq - 2)

    def share(shift):
        return remote(
            own.at[0], own.at[shift], ksend.at[shift - 1], krecv.at[shift - 1],
            {"seq": (seq + shift) % n_seq},
        )

    for shift in range(1, n_seq):
        share(shift).start()
    down_out.start()
    for i in range(SLABS):
        slab_in(i).wait()

        @pl.loop(0, slab // 256)
        def _(j):
            at = pl.ds(pl.multiple_of(i * slab + j * 256, 256), 256)
            wgu[0, :, at] = jnp.swapaxes(wraw[at], 0, 1)

        slab_out(i).start()

    idt = idt_ref[...]
    top_count = idt.shape[0]
    kinds_t = lax.broadcasted_iota(jnp.int32, (experts, rows), 0)
    hot_t = [(idt[k : k + 1, :] == kinds_t).astype(F32) for k in range(top_count)]
    down = lax.broadcasted_iota(jnp.int32, (rows, rows), 0)
    along = lax.broadcasted_iota(jnp.int32, (rows, rows), 1)
    before_t = jnp.dot(
        sum(hot_t).astype(BF16), (down < along).astype(F32).astype(BF16), preferred_element_type=F32
    )
    meta[...] = jnp.zeros_like(meta)
    for k in range(top_count):
        slot_t = jnp.sum(before_t * hot_t[k], axis=0, keepdims=True)
        meta[k : k + 1, :] = idt[k : k + 1, :].astype(F32) * float(cap) + slot_t

    for shift in range(1, n_seq):
        share(shift).wait_recv()
    for offset in range(n_branch - 1):
        picked[offset] = own[(seq - list_ref[offset] + n_seq) % n_seq]

    def lend(offset):
        return remote(
            picked.at[offset], sib.at[offset], ssend.at[offset], srecv.at[offset],
            {"branch": (branch + offset + 1) % n_branch},
        )

    for offset in range(n_branch - 1):
        lend(offset).start()

    def chunk(r):
        return pl.ds(pl.multiple_of(r * span, span), span)

    def columns(head, half):
        base = (head * group + half * pack) * HEAD_SIZE
        return [slice(base + i * HEAD_SIZE, base + (i + 1) * HEAD_SIZE) for i in range(pack)]

    def kv_cols(head):
        return (
            slice(head * HEAD_SIZE, (head + 1) * HEAD_SIZE),
            slice((kv_heads + head) * HEAD_SIZE, (kv_heads + head + 1) * HEAD_SIZE),
        )

    tall = pack * span

    @pl.loop(0, CHUNKS)
    def _(r):
        at_row = r * span + lax.broadcasted_iota(jnp.int32, (tall, own_len), 0) % span
        at_col = lax.broadcasted_iota(jnp.int32, (tall, own_len), 1)
        earlier = at_col // rows
        bias = jnp.where(
            earlier == 0,
            jnp.where(at_col <= at_row, 0.0, -1e30),
            jnp.where(earlier <= seq, 0.0, -1e30),
        )
        for head in range(kv_heads):
            kcol, vcol = kv_cols(head)
            for half in range(halves):
                cols = columns(head, half)
                q = jnp.concatenate([q_ref[chunk(r), c] for c in cols], axis=0)
                keys = own[:, :, kcol].reshape(own_len, HEAD_SIZE)
                values = own[:, :, vcol].reshape(own_len, HEAD_SIZE)
                scores = lax.dot_general(q, keys, nt, preferred_element_type=F32) * scale + bias
                top = jnp.max(scores, axis=1, keepdims=True)
                p = jnp.exp(scores - top)
                tops[r, head * halves + half] = top
                totals[r, head * halves + half] = jnp.sum(p, axis=1, keepdims=True)
                mixed = jnp.dot(p.astype(BF16), values, preferred_element_type=F32)
                for i, c in enumerate(cols):
                    state[chunk(r), c] = mixed[i * span : (i + 1) * span]

    for offset in range(n_branch - 1):
        lend(offset).wait_recv()

    def rows_out(r):
        return remote(
            norm.at[chunk(r)], raw.at[inner, chunk(r)], rowsend.at[r], rowrecv.at[inner, r],
            {"branch": onward},
        )

    @pl.loop(0, CHUNKS)
    def _(r):
        for head in range(kv_heads):
            kcol, vcol = kv_cols(head)
            for half in range(halves):
                cols = columns(head, half)
                q = jnp.concatenate([q_ref[chunk(r), c] for c in cols], axis=0)
                keys = sib[:, :, kcol].reshape(sib_len, HEAD_SIZE)
                values = sib[:, :, vcol].reshape(sib_len, HEAD_SIZE)
                scores = lax.dot_general(q, keys, nt, preferred_element_type=F32) * scale
                own_top = tops[r, head * halves + half]
                top = jnp.maximum(own_top, jnp.max(scores, axis=1, keepdims=True))
                p = jnp.exp(scores - top)
                shrink = jnp.exp(own_top - top)
                total = totals[r, head * halves + half] * shrink + jnp.sum(p, axis=1, keepdims=True)
                mixed = jnp.dot(p.astype(BF16), values, preferred_element_type=F32)
                inverse = 1.0 / total
                for i, c in enumerate(cols):
                    at = slice(i * span, (i + 1) * span)
                    context = (state[chunk(r), c] * shrink[at] + mixed[at]) * inverse[at]
                    state[chunk(r), c] = res_ref[chunk(r), c].astype(F32) + context.astype(BF16).astype(F32)
        full = state[chunk(r), :]
        norm[chunk(r), :] = (
            full * lax.rsqrt(jnp.mean(full * full, axis=1, keepdims=True) + 1e-06)
        ).astype(BF16)
        rows_out(r).start()

    logits_t = lax.dot_general(router_ref[...], norm[...], nt, preferred_element_type=F32)
    chosen_t = [jnp.sum(logits_t * hot_t[k], axis=0, keepdims=True) for k in range(top_count)]
    for k in range(top_count):
        meta[top_count + k : top_count + k + 1, :] = 1.0 / sum(
            jnp.exp(c - chosen_t[k]) for c in chosen_t
        )

    def meta_out():
        return remote(meta, xmeta.at[inner], msend.at[0], mrecv.at[inner], {"branch": onward})

    meta_out().start()

    def relay(c):
        return remote(
            raw.at[0, :, part(c)], raw.at[2, :, part(c)], relsend.at[c], relrecv.at[c], {"branch": far}
        )

    def meta_relay():
        return remote(xmeta.at[0], xmeta.at[2], msend.at[1], mrecv.at[2], {"branch": far})

    def meta_of(g):
        return meta[...] if g == 0 else xmeta[g - 1]

    def slots_of(g, count):
        where = lax.broadcasted_iota(jnp.int32, (cap, rows), 0).astype(F32)
        given = meta_of(g)
        return given, [where + (holders[f] * cap).astype(F32) for f in range(count)]

    def picks(g, count):
        given, where = slots_of(g, count)
        return jnp.concatenate(
            [(given[0:1] == w).astype(F32) + (given[1:2] == w).astype(F32) for w in where], axis=0
        ).astype(BF16)

    def shares(g, count):
        given, where = slots_of(g, count)
        weight = jnp.concatenate(
            [
                jnp.where(given[0:1] == w, given[2:3], 0.0) + jnp.where(given[1:2] == w, given[3:4], 0.0)
                for w in where
            ],
            axis=0,
        ).T
        high = weight.astype(BF16)
        return high, (weight - high.astype(F32)).astype(BF16)

    def spot(g, f):
        if f == 1:
            return g, 1
        return (1 if g == 0 else g), f - 2

    def forward(g, f, c):
        tg, th = spot(g, f)
        return remote(
            fwd.at[g, f - 1, :, part(c)], recv.at[tg, th, :, part(c)],
            fsend.at[g, f - 1], drecv.at[tg, th], places[f],
        )

    def give(g, count, pick, c):
        source = norm[:, part(c)] if g == 0 else raw[g - 1, :, part(c)]
        taken = jnp.dot(pick, source, preferred_element_type=F32).astype(BF16)
        recv[g, 0, :, part(c)] = taken[:cap]
        for f in range(1, count):
            fwd[g, f - 1, :, part(c)] = taken[f * cap : (f + 1) * cap]
        for f in ((3, 2, 1) if count == 4 else (1,)):
            forward(g, f, c).start()

    def give_all(g, count):
        pick = picks(g, count)
        for c in range(PARTS):
            give(g, count, pick, c)

    def whole(g, h):
        return remote(recv.at[g, h], recv.at[g, h], fsend.at[0, 0], drecv.at[g, h], places[1])

    def back_to(g, c):
        return remote(
            res.at[g, 1, :, part(c)], back.at[g, 0, :, part(c)],
            bsend.at[g, 1], brecv.at[g, 0, c], places[1],
        )

    def down_line(g, c):
        slot = g // 2 * g
        return remote(
            res.at[g, 0, :, part(c)], back.at[slot, 1, :, part(c)],
            bsend.at[g, 0], brecv.at[slot, 1, c], places[2],
        )

    def pass_on(g, c):
        slot = g // 2 * g
        return remote(
            back.at[g, 0, :, part(c)], back.at[slot, 2, :, part(c)],
            lsend.at[g - 1], brecv.at[slot, 2, c], places[2],
        )

    def compute(g, first=False):
        whole(g, 1).wait_recv()
        if not first:
            pl.when(inner == 0)(lambda: whole(g, 0).wait_recv())
        x = recv[g].reshape(2 * cap, width)
        acts = []
        for h in range(2):
            gate = jnp.dot(x, wgu[h, 0], preferred_element_type=F32)
            up = jnp.dot(x, wgu[h, 1], preferred_element_type=F32)
            acts.append((gate / (1.0 + jnp.exp(-gate)) * up).astype(BF16))
        for c in range(PARTS):
            done = jnp.dot(acts[0], wdn[0, :, part(c)], preferred_element_type=F32)
            done += jnp.dot(acts[1], wdn[1, :, part(c)], preferred_element_type=F32)
            res[g, :, :, part(c)] = done.astype(BF16).reshape(2, cap, step)
            back_to(g, c).start()

    def pass_all(g):
        if g == 1:
            for c in range(PARTS):
                down_line(g, c).start()
        for c in range(PARTS):
            back_to(g, c).wait_recv()
            if g > 1:
                down_line(g, c).start()
            pass_on(g, c).start()

    def combined(g, count, weight, c):
        for f in range(count - 1):
            remote(
                back.at[g, f, :, part(c)], back.at[g, f, :, part(c)],
                bsend.at[0, 0], brecv.at[g, f, c], places[1],
            ).wait_recv()
        given = jnp.concatenate(
            [res[g, 0, :, part(c)]] + [back[g, f, :, part(c)] for f in range(count - 1)], axis=0
        )
        return jnp.dot(weight[0], given, preferred_element_type=F32) + jnp.dot(
            weight[1], given, preferred_element_type=F32
        )

    def result(s, c):
        if s == 2:
            return remote(xout.at[2, c], fin.at[0, c], osend.at[2, c], orecv.at[0, c], {"branch": near})
        return remote(xout.at[s, c], fin.at[s, c], osend.at[s, c], orecv.at[s, c], {"branch": far})

    def wait_rows(g):
        remote(xmeta.at[g - 1], xmeta.at[g - 1], msend.at[0], mrecv.at[g - 1], places[2]).wait_recv()
        if g < 3:
            for r in range(CHUNKS):
                at = slice(r * span, (r + 1) * span)
                remote(
                    raw.at[g - 1, at], raw.at[g - 1, at], rowsend.at[0], rowrecv.at[g - 1, r], places[2]
                ).wait_recv()

    is_inner = pl.when(inner == 1)
    is_outer = pl.when(inner == 0)

    is_inner(lambda: give_all(0, 4))
    is_outer(lambda: give_all(0, 2))

    for i in range(SLABS):
        slab_out(i).wait_recv()
    down_out.wait_recv()
    down_in.wait()

    is_inner(lambda: compute(0, True))

    def far_rows(c, pick):
        remote(
            raw.at[2, :, part(c)], raw.at[2, :, part(c)], relsend.at[0], relrecv.at[c], places[2]
        ).wait_recv()
        give(3, 4, pick, c)

    @is_inner
    def _():
        wait_rows(1)
        meta_relay().start()
        for c in range(PARTS):
            relay(c).start()
        wait_rows(2)
        give_all(2, 4)
        wait_rows(3)
        far_rows(0, picks(3, 4))

    compute(1 + inner)
    is_outer(lambda: pass_all(1))

    def send_far(s, span):
        weight = shares(2 + s, 4)
        for c in span:
            xout[s, c] = combined(2 + s, 4, weight, c).astype(BF16)
            result(s, c).start()

    def settle(count):
        weight = shares(0, count)
        for c in range(PARTS):
            state[:, part(c)] += combined(0, count, weight, c)

    @is_inner
    def _():
        pick = picks(3, 4)
        for c in range(1, PARTS):
            far_rows(c, pick)
        give_all(1, 2)
        send_far(0, range(PARTS // 2))

    compute(2 + inner)
    is_inner(lambda: send_far(0, range(PARTS // 2, PARTS)))
    is_outer(lambda: pass_all(2))
    compute(3 - 2 * inner)

    def arrived(s, c):
        remote(fin.at[s, c], fin.at[s, c], osend.at[0, 0], orecv.at[s, c], places[2]).wait_recv()

    @is_inner
    def _():
        settle(4)
        send_far(1, range(PARTS))
        weight = shares(1, 2)
        for c in range(PARTS):
            partial = combined(1, 2, weight, c)
            arrived(1, c)
            xout[2, c] = (partial + fin[1, c].astype(F32)).astype(BF16)
            result(2, c).start()

    @is_outer
    def _():
        pass_all(3)
        compute(0, True)
        settle(2)

    for c in range(PARTS):
        arrived(0, c)
        out_ref[:, part(c)] = (state[:, part(c)] + fin[0, c].astype(F32)).astype(BF16)

    for shift in range(1, n_seq):
        share(shift).wait_send()
    for i in range(SLABS):
        slab_out(i).wait_send()
    down_out.wait_send()
    for offset in range(n_branch - 1):
        lend(offset).wait_send()
    for r in range(CHUNKS):
        rows_out(r).wait_send()
    meta_out().wait_send()

    def sent(g, f):
        remote(fwd.at[g, f - 1], fwd.at[g, f - 1], fsend.at[g, f - 1], drecv.at[0, 0], places[1]).wait_send()

    def returned(g, h):
        remote(res.at[g, h], res.at[g, h], bsend.at[g, h], brecv.at[0, 0, 0], places[1]).wait_send()

    sent(0, 1)
    for g in range(4):
        returned(g, 1)

    @is_inner
    def _():
        for g in (0, 2, 3):
            for f in ((2, 3) if g == 0 else (1, 2, 3)):
                sent(g, f)
        sent(1, 1)
        for c in range(PARTS):
            relay(c).wait_send()
            for s in range(3):
                result(s, c).wait_send()
        meta_relay().wait_send()

    @is_outer
    def _():
        for g in (1, 2, 3):
            returned(g, 0)
            remote(back.at[g, 0], back.at[g, 0], lsend.at[g - 1], brecv.at[0, 0, 0], places[2]).wait_send()


def run_line(listed, q, kv, residual, router_t, idt, wgu, wdn, experts, cap, n_branch, n_seq):
    rows, width = q.shape
    ff = wdn.shape[0]
    kv_width = kv.shape[1] * kv.shape[2]
    part = width // PARTS
    tall = 2 * rows
    steps = width // HEAD_SIZE * rows // tall // CHUNKS
    dma = pltpu.SemaphoreType.DMA
    return pl.pallas_call(
        functools.partial(line_kernel, experts, cap, n_branch, n_seq),
        out_shape=jax.ShapeDtypeStruct((rows, width), BF16),
        in_specs=[SMEM] + [VMEM] * 5 + [ANY, ANY],
        out_specs=VMEM,
        scratch_shapes=[
            pltpu.VMEM((n_seq, rows, kv_width), BF16),
            pltpu.VMEM((n_branch - 1, rows, kv_width), BF16),
            pltpu.VMEM((n_branch - 1, rows, kv_width), BF16),
            pltpu.VMEM((CHUNKS, steps, tall, 1), F32),
            pltpu.VMEM((CHUNKS, steps, tall, 1), F32),
            pltpu.VMEM((rows, width), F32),
            pltpu.VMEM((rows, width), BF16),
            pltpu.VMEM((3, rows, width), BF16),
            pltpu.VMEM((8, rows), F32),
            pltpu.VMEM((3, 8, rows), F32),
            pltpu.VMEM((4, 2, cap, width), BF16),
            pltpu.VMEM((4, 2, cap, width), BF16),
            pltpu.VMEM((4, 3, cap, width), BF16),
            pltpu.VMEM((4, 3, cap, width), BF16),
            pltpu.VMEM((width, 2, ff), BF16),
            pltpu.VMEM((2, 2, width, ff), BF16),
            pltpu.VMEM((2, ff, width), BF16),
            pltpu.VMEM((3, PARTS, rows, part), BF16),
            pltpu.VMEM((2, PARTS, rows, part), BF16),
            dma((n_seq - 1,)), dma((n_seq - 1,)), dma((n_branch - 1,)), dma((n_branch - 1,)),
            dma((SLABS + 1,)), dma((SLABS + 1,)), dma((SLABS + 1,)),
            dma((CHUNKS,)), dma((2, CHUNKS)), dma((PARTS,)), dma((PARTS,)), dma((2,)), dma((3,)),
            dma((4, 3)), dma((4, 2)), dma((4, 2)), dma((4, 3, PARTS)), dma((3,)), dma((3, PARTS)), dma((2, PARTS)),
        ],
        compiler_params=pltpu.CompilerParams(
            collective_id=2, has_side_effects=True, vmem_limit_bytes=LINE_VMEM_LIMIT
        ),
    )(listed, q, kv, residual, router_t, idt, wgu, wdn)


def on_device(
    n_branch, n_seq, queries, keyvals, residual, read_list, router, expert_ids, w_gate_up, w_down
):
    rows = queries.shape[1]
    experts = router.shape[1]
    top_count = expert_ids.shape[2]
    capacity = 2 * ((3 * rows * top_count + 4 * experts - 1) // (4 * experts))
    cap = (capacity + 15) // 16 * 16
    if n_branch == 4 and n_seq == 4 and experts == 8 and top_count == 2:
        return run_line(
            read_list.reshape(-1), queries[0], keyvals[0], residual[0], router.T, expert_ids[0].T,
            w_gate_up[0], w_down[0], experts, cap, n_branch, n_seq,
        )[None]
    kv = keyvals.reshape(rows, -1)
    wgu = jnp.swapaxes(w_gate_up[0], 0, 1)
    shifts = [
        lax.ppermute(kv, "seq", [(i, (i + step) % n_seq) for i in range(n_seq)])
        for step in range(1, n_seq)
    ]
    own = jnp.stack([kv] + shifts)
    send, state, gate, normed, meta = attend(
        read_list.reshape(-1), queries[0], own, residual[0], router.T, expert_ids[0],
        experts, experts, cap, n_branch, n_seq,
    )
    return run_experts(send, state, gate, wgu, w_down[0], experts, cap, n_seq)[None]


def solution(mesh):
    return jax.shard_map(
        functools.partial(on_device, mesh.shape["branch"], mesh.shape["seq"]),
        mesh=mesh,
        in_specs=(
            P(("rollout", "branch"), "seq", None),
            P(("rollout", "branch"), "seq", None, None),
            P(("rollout", "branch"), "seq", None),
            P(("rollout", "branch"), "seq", None),
            P(),
            P(("rollout", "branch"), "seq", None),
            P(("branch", "seq"), None, None, None),
            P(("branch", "seq"), None, None),
        ),
        out_specs=P(("rollout", "branch"), "seq", None),
        check_vma=False,
    )
```

```python
import functools
import math

import jax
import jax.numpy as jnp
from jax import lax
from jax.experimental import pallas as pl
from jax.experimental.pallas import tpu as pltpu
from jax.sharding import PartitionSpec as P

HEAD_SIZE = 128
PARTS = 8
CHUNKS = 8
SLABS = 4
VMEM_LIMIT = 60 * 1024 * 1024
LINE_VMEM_LIMIT = 63 * 1024 * 1024
F32 = jnp.float32
BF16 = jnp.bfloat16
ANY = pl.BlockSpec(memory_space=pl.ANY)
VMEM = pl.BlockSpec(memory_space=pltpu.VMEM)
SMEM = pl.BlockSpec(memory_space=pltpu.SMEM)


def flipped(number, mask, count):
    value, bit = 0, 1
    while bit < count:
        value = value + ((number // bit + mask // bit) % 2) * bit
        bit *= 2
    return value


def attend_kernel(
    experts, cap, n_branch, n_seq,
    list_ref, q_ref, own_ref, res_ref, router_ref, ids_ref, idt_ref,
    send_ref, state_ref, gate_ref, norm_ref, meta_ref,
    picked, sib_ref, tops, totals, ssem, rsem,
):
    branch = lax.axis_index("branch")
    seq = lax.axis_index("seq")
    me = (branch * n_seq + seq) // 2
    rows, width = q_ref.shape
    kv_heads = own_ref.shape[2] // (2 * HEAD_SIZE)
    group = width // HEAD_SIZE // kv_heads
    together = 2
    tall = together * rows
    own_len = n_seq * rows
    sib_len = (n_branch - 1) * rows
    scale = 1.0 / math.sqrt(HEAD_SIZE)
    nt = (((1,), (1,)), ((), ()))

    barrier = pltpu.get_barrier_semaphore()
    for step in range(1, n_branch):
        pl.semaphore_signal(
            barrier, inc=1, device_id={"branch": (branch + step) % n_branch},
            device_id_type=pl.DeviceIdType.MESH,
        )
    for offset in range(n_branch - 1):
        picked[offset] = own_ref[(seq - list_ref[offset] + n_seq) % n_seq]
    pl.semaphore_wait(barrier, n_branch - 1)
    copies = []
    for offset in range(n_branch - 1):
        copy = pltpu.make_async_remote_copy(
            src_ref=picked.at[offset], dst_ref=sib_ref.at[offset],
            send_sem=ssem.at[offset], recv_sem=rsem.at[offset],
            device_id={"branch": (branch + offset + 1) % n_branch},
            device_id_type=pl.DeviceIdType.MESH,
        )
        copy.start()
        copies.append(copy)

    at_row = lax.broadcasted_iota(jnp.int32, (tall, own_len), 0) % rows
    at_col = lax.broadcasted_iota(jnp.int32, (tall, own_len), 1)
    earlier = at_col // rows
    bias = jnp.where(
        earlier == 0,
        jnp.where(at_col <= at_row, 0.0, -1e30),
        jnp.where(earlier <= seq, 0.0, -1e30),
    )

    def head_parts(head, step):
        base = (head * group + step * together) * HEAD_SIZE
        cols = [
            pl.ds(pl.multiple_of(base + i * HEAD_SIZE, HEAD_SIZE), HEAD_SIZE)
            for i in range(together)
        ]
        return cols, jnp.concatenate([q_ref[:, c] for c in cols], axis=0)

    def kv_cols(head):
        return (
            slice(head * HEAD_SIZE, (head + 1) * HEAD_SIZE),
            slice((kv_heads + head) * HEAD_SIZE, (kv_heads + head + 1) * HEAD_SIZE),
        )

    steps = group // together
    for head in range(kv_heads):
        kcol, vcol = kv_cols(head)

        @pl.loop(0, steps)
        def _(step):
            cols, q = head_parts(head, step)
            keys = own_ref[:, :, kcol].reshape(own_len, HEAD_SIZE)
            values = own_ref[:, :, vcol].reshape(own_len, HEAD_SIZE)
            scores = lax.dot_general(q, keys, nt, preferred_element_type=F32) * scale + bias
            top = jnp.max(scores, axis=1, keepdims=True)
            p = jnp.exp(scores - top)
            tops[head * steps + step] = top
            totals[head * steps + step] = jnp.sum(p, axis=1, keepdims=True)
            mixed = jnp.dot(p.astype(BF16), values, preferred_element_type=F32)
            for i, c in enumerate(cols):
                state_ref[:, c] = mixed[i * rows : (i + 1) * rows]

    for copy in copies:
        copy.wait()
    for head in range(kv_heads):
        kcol, vcol = kv_cols(head)

        @pl.loop(0, steps)
        def _(step):
            cols, q = head_parts(head, step)
            keys = sib_ref[:, :, kcol].reshape(sib_len, HEAD_SIZE)
            values = sib_ref[:, :, vcol].reshape(sib_len, HEAD_SIZE)
            scores = lax.dot_general(q, keys, nt, preferred_element_type=F32) * scale
            own_top = tops[head * steps + step]
            top = jnp.maximum(own_top, jnp.max(scores, axis=1, keepdims=True))
            p = jnp.exp(scores - top)
            shrink = jnp.exp(own_top - top)
            total = totals[head * steps + step] * shrink + jnp.sum(p, axis=1, keepdims=True)
            mixed = jnp.dot(p.astype(BF16), values, preferred_element_type=F32)
            inverse = 1.0 / total
            for i, c in enumerate(cols):
                part = slice(i * rows, (i + 1) * rows)
                context = (state_ref[:, c] * shrink[part] + mixed[part]) * inverse[part]
                state_ref[:, c] = res_ref[:, c].astype(F32) + context.astype(BF16).astype(F32)

    state = state_ref[...]
    normed = (
        state * lax.rsqrt(jnp.mean(state * state, axis=1, keepdims=True) + 1e-06)
    ).astype(BF16)
    logits = lax.dot_general(normed, router_ref[...], nt, preferred_element_type=F32)

    top_count = ids_ref.shape[1]
    ids, idt = ids_ref[...], idt_ref[...]
    kinds = lax.broadcasted_iota(jnp.int32, (rows, experts), 1)
    kinds_t = lax.broadcasted_iota(jnp.int32, (experts, rows), 0)
    hot = [(ids[:, k : k + 1] == kinds).astype(F32) for k in range(top_count)]
    hot_t = [(idt[k : k + 1, :] == kinds_t).astype(F32) for k in range(top_count)]
    down = lax.broadcasted_iota(jnp.int32, (rows, rows), 0)
    along = lax.broadcasted_iota(jnp.int32, (rows, rows), 1)
    before = jnp.dot((along < down).astype(F32).astype(BF16), sum(hot).astype(BF16), preferred_element_type=F32)
    before_t = jnp.dot(sum(hot_t).astype(BF16), (down < along).astype(F32).astype(BF16), preferred_element_type=F32)
    dest, dest_t = [], []
    for k in range(top_count):
        slot = jnp.sum(before * hot[k], axis=1, keepdims=True).astype(jnp.int32)
        dest.append((ids[:, k : k + 1] ^ me) * cap + slot)
        slot_t = jnp.sum(before_t * hot_t[k], axis=0, keepdims=True).astype(jnp.int32)
        dest_t.append((idt[k : k + 1, :] ^ me) * cap + slot_t)
    chosen = [jnp.sum(logits * hot[k], axis=1, keepdims=True) for k in range(top_count)]
    gates = [1.0 / sum(jnp.exp(c - chosen[k]) for c in chosen) for k in range(top_count)]

    parts, _, part_width = norm_ref.shape
    for c in range(parts):
        norm_ref[c] = normed[:, c * part_width : (c + 1) * part_width]
    logits_t = lax.dot_general(router_ref[...], normed, nt, preferred_element_type=F32)
    chosen_t = [jnp.sum(logits_t * hot_t[k], axis=0, keepdims=True) for k in range(top_count)]
    meta_ref[...] = jnp.zeros_like(meta_ref)
    for k in range(top_count):
        meta_ref[k : k + 1, :] = dest_t[k].astype(F32)
        meta_ref[top_count + k : top_count + k + 1, :] = 1.0 / sum(
            jnp.exp(c - chosen_t[k]) for c in chosen_t
        )

    pair = 2 * cap
    places = lax.broadcasted_iota(jnp.int32, (rows, pair), 1)
    places_t = lax.broadcasted_iota(jnp.int32, (pair, rows), 0)
    for p in range(send_ref.shape[0] // pair):
        pick = sum((dest_t[k] - p * pair == places_t).astype(F32) for k in range(top_count))
        send_ref[p * pair : (p + 1) * pair, :] = jnp.dot(
            pick.astype(BF16), normed, preferred_element_type=F32
        ).astype(BF16)
        weight = sum(
            jnp.where(dest[k] - p * pair == places, gates[k], 0.0) for k in range(top_count)
        )
        high = weight.astype(BF16)
        gate_ref[p, 0] = high
        gate_ref[p, 1] = (weight - high.astype(F32)).astype(BF16)


def attend(listed, q, own, residual, router_t, ids, experts, near, cap, n_branch, n_seq):
    rows, width = q.shape
    halves = width // HEAD_SIZE // 2
    return pl.pallas_call(
        functools.partial(attend_kernel, experts, cap, n_branch, n_seq),
        out_shape=(
            jax.ShapeDtypeStruct((near * cap, width), BF16),
            jax.ShapeDtypeStruct((rows, width), F32),
            jax.ShapeDtypeStruct((near // 2, 2, rows, 2 * cap), BF16),
            jax.ShapeDtypeStruct((PARTS, rows, width // PARTS), BF16),
            jax.ShapeDtypeStruct((8, rows), F32),
        ),
        in_specs=[SMEM] + [VMEM] * 6,
        out_specs=(VMEM,) * 5,
        scratch_shapes=[
            pltpu.VMEM((n_branch - 1, rows, own.shape[2]), BF16),
            pltpu.VMEM((n_branch - 1, rows, own.shape[2]), BF16),
            pltpu.VMEM((halves, 2 * rows, 1), F32),
            pltpu.VMEM((halves, 2 * rows, 1), F32),
            pltpu.SemaphoreType.DMA((n_branch,)),
            pltpu.SemaphoreType.DMA((n_branch,)),
        ],
        compiler_params=pltpu.CompilerParams(
            collective_id=0, has_side_effects=True, vmem_limit_bytes=VMEM_LIMIT
        ),
    )(listed, q, own, residual, router_t, ids, ids.T)


def expert_kernel(
    experts, cap, n_seq,
    send_ref, state_ref, gate_ref, wgu_ref, wdn_ref, out_ref,
    recv, res, ret, wgu, wdn, acc,
    wsend, wrecv, wloc, lsem, dsend, drecv, bsend, brecv,
):
    branch = lax.axis_index("branch")
    seq = lax.axis_index("seq")
    core = seq % 2
    me = (branch * n_seq + seq) // 2
    pair = 2 * cap
    width = send_ref.shape[1]
    twin = {"seq": seq + 1 - 2 * core}
    mesh_id = pl.DeviceIdType.MESH

    def place(k):
        other = flipped(me, k, experts)
        return {"branch": (2 * other) // n_seq, "seq": (2 * other) % n_seq + core}

    barrier = pltpu.get_barrier_semaphore()
    pl.semaphore_signal(barrier, inc=1, device_id=twin, device_id_type=mesh_id)

    @pl.loop(1, experts)
    def _(k):
        pl.semaphore_signal(barrier, inc=1, device_id=place(k), device_id_type=mesh_id)

    pl.semaphore_wait(barrier, experts)

    def block(k):
        return pl.ds(pl.multiple_of(k * cap, 16), cap)

    def dispatch(k):
        return pltpu.make_async_remote_copy(
            src_ref=send_ref.at[block(k)], dst_ref=recv.at[block(k)],
            send_sem=dsend.at[k], recv_sem=drecv.at[k],
            device_id=place(k), device_id_type=mesh_id,
        )

    def give_back(k):
        return pltpu.make_async_remote_copy(
            src_ref=res.at[block(k)], dst_ref=ret.at[block(k)],
            send_sem=bsend.at[k], recv_sem=brecv.at[k],
            device_id=place(k), device_id_type=mesh_id,
        )

    weights = []
    for i, (src, dst) in enumerate(((wgu_ref, wgu), (wdn_ref, wdn))):
        weights.append(
            pltpu.make_async_remote_copy(
                src_ref=src, dst_ref=dst.at[1], send_sem=wsend.at[i], recv_sem=wrecv.at[i],
                device_id=twin, device_id_type=mesh_id,
            )
        )
        weights.append(pltpu.make_async_copy(src, dst.at[0], wloc.at[i]))
    dispatch(1).start()
    mine = pltpu.make_async_copy(send_ref.at[block(0)], recv.at[block(0)], lsem)
    mine.start()

    @pl.loop(experts // 2, experts)
    def _(k):
        dispatch(k).start()

    @pl.loop(2, experts // 2)
    def _(k):
        dispatch(k).start()

    for copy in weights:
        copy.start()
    acc[...] = state_ref[...]
    for copy in weights:
        copy.wait()

    chunk = 512

    def compute(p):
        span = pl.ds(pl.multiple_of(p * pair, 16), pair)
        acts = []
        for h in range(2):
            x = recv[span, :]
            gate = jnp.dot(x, wgu[h, 0], preferred_element_type=F32)
            up = jnp.dot(x, wgu[h, 1], preferred_element_type=F32)
            acts.append((gate / (1.0 + jnp.exp(-gate)) * up).astype(BF16))
        for start in range(0, width, chunk):
            cols = slice(start, start + chunk)
            done = jnp.dot(acts[0], wdn[0, :, cols], preferred_element_type=F32)
            done += jnp.dot(acts[1], wdn[1, :, cols], preferred_element_type=F32)
            res[span, cols] = done.astype(BF16)

    quarter = experts // 4

    def turn(i):
        return jnp.where(i <= quarter, i + quarter - 1, i - quarter)

    mine.wait()
    dispatch(1).wait_recv()
    compute(0)
    give_back(1).start()

    @pl.loop(1, experts // 2)
    def _(i):
        p = turn(i)
        dispatch(2 * p).wait_recv()
        dispatch(2 * p + 1).wait_recv()
        compute(p)
        give_back(2 * p).start()
        give_back(2 * p + 1).start()

    def add(p, rows):
        for start in range(0, width, chunk):
            cols = slice(start, start + chunk)
            block_rows = rows(cols)
            acc[:, cols] += jnp.dot(
                gate_ref[p, 0], block_rows, preferred_element_type=F32
            ) + jnp.dot(gate_ref[p, 1], block_rows, preferred_element_type=F32)

    give_back(1).wait_recv()
    add(0, lambda cols: jnp.concatenate([res[0:cap, cols], ret[cap:pair, cols]], axis=0))

    @pl.loop(1, experts // 2)
    def _(i):
        p = turn(i)
        give_back(2 * p).wait_recv()
        give_back(2 * p + 1).wait_recv()
        span = pl.ds(pl.multiple_of(p * pair, 16), pair)
        add(p, lambda cols: ret[span, cols])

    out_ref[...] = acc[...].astype(BF16)

    @pl.loop(1, experts)
    def _(k):
        dispatch(k).wait_send()
        give_back(k).wait_send()


def run_experts(send, state, gate, wgu, wdn, experts, cap, n_seq):
    rows, width = state.shape
    ff = wdn.shape[0]
    return pl.pallas_call(
        functools.partial(expert_kernel, experts, cap, n_seq),
        out_shape=jax.ShapeDtypeStruct((rows, width), BF16),
        in_specs=[ANY, VMEM, VMEM, ANY, ANY],
        out_specs=VMEM,
        scratch_shapes=[
            pltpu.VMEM((experts * cap, width), BF16),
            pltpu.VMEM((experts * cap, width), BF16),
            pltpu.VMEM((experts * cap, width), BF16),
            pltpu.VMEM((2, 2, width, ff), BF16),
            pltpu.VMEM((2, ff, width), BF16),
            pltpu.VMEM((rows, width), F32),
            pltpu.SemaphoreType.DMA((2,)),
            pltpu.SemaphoreType.DMA((2,)),
            pltpu.SemaphoreType.DMA((2,)),
            pltpu.SemaphoreType.DMA,
            pltpu.SemaphoreType.DMA((experts,)),
            pltpu.SemaphoreType.DMA((experts,)),
            pltpu.SemaphoreType.DMA((experts,)),
            pltpu.SemaphoreType.DMA((experts,)),
        ],
        compiler_params=pltpu.CompilerParams(
            collective_id=1, has_side_effects=True, vmem_limit_bytes=VMEM_LIMIT
        ),
    )(send, state, gate, wgu, wdn)


def line_kernel(
    experts, cap, n_branch, n_seq,
    list_ref, q_ref, kv_ref, res_ref, router_ref, idt_ref, wgu_ref, wdn_ref,
    out_ref,
    own, picked, sib, tops, totals, state, norm, raw, meta, xmeta,
    recv, res, back, fwd, wraw, wgu, wdn, xout, fin, done,
    ksend, krecv, ssend, srecv, wsend, wrecv, wloc,
    rowsend, rowrecv, relsend, relrecv, msend, mrecv,
    fsend, drecv, bsend, brecv, lsend, osend, orecv, dsend,
):
    branch = lax.axis_index("branch")
    seq = lax.axis_index("seq")
    inner = (branch + 1) // 2 % 2
    mesh_id = pl.DeviceIdType.MESH
    rows, width = q_ref.shape
    kv_heads = own.shape[2] // (2 * HEAD_SIZE)
    group = width // HEAD_SIZE // kv_heads
    own_len = n_seq * rows
    sib_len = (n_branch - 1) * rows
    scale = 1.0 / math.sqrt(HEAD_SIZE)
    nt = (((1,), (1,)), ((), ()))
    step = width // PARTS
    span = rows // CHUNKS
    pack = 2 * rows // span
    halves = group // pack

    across = (seq + 2) % n_seq
    near = branch + 1 - 2 * (branch % 2)
    far = n_branch - 1 - branch
    onward = near + inner * (far - near)
    places = [
        {"branch": branch, "seq": seq},
        {"branch": branch, "seq": across},
        {"branch": near, "seq": seq},
        {"branch": near, "seq": across},
    ]
    holders = [(p["branch"] * n_seq + p["seq"]) // 2 for p in places]

    def remote(src, dst, send, arrive, device):
        return pltpu.make_async_remote_copy(
            src_ref=src, dst_ref=dst, send_sem=send, recv_sem=arrive,
            device_id=device, device_id_type=mesh_id,
        )

    def part(c):
        return slice(c * step, (c + 1) * step)

    twin = {"seq": seq + 1 - 2 * (seq % 2)}
    slab = width // SLABS

    def slab_in(i):
        at = slice(i * slab, (i + 1) * slab)
        return pltpu.make_async_copy(wgu_ref.at[at], wraw.at[at], wloc.at[i])

    def slab_out(i):
        at = slice(i * slab, (i + 1) * slab)
        return remote(wgu.at[0, :, at], wgu.at[1, :, at], wsend.at[i], wrecv.at[i], twin)

    down_in = pltpu.make_async_copy(wdn_ref, wdn.at[0], wloc.at[SLABS])
    down_out = remote(wdn_ref, wdn.at[1], wsend.at[SLABS], wrecv.at[SLABS], twin)
    for i in range(SLABS):
        slab_in(i).start()
    down_in.start()
    own[0] = kv_ref[...].reshape(rows, own.shape[2])

    barrier = pltpu.get_barrier_semaphore()
    for shift in range(1, n_branch):
        pl.semaphore_signal(
            barrier, inc=1, device_id={"branch": (branch + shift) % n_branch}, device_id_type=mesh_id
        )
    for shift in range(1, n_seq):
        pl.semaphore_signal(
            barrier, inc=1, device_id={"seq": (seq + shift) % n_seq}, device_id_type=mesh_id
        )
    pl.semaphore_wait(barrier, n_branch + n_seq - 2)

    def share(shift):
        return remote(
            own.at[0], own.at[shift], ksend.at[shift - 1], krecv.at[shift - 1],
            {"seq": (seq + shift) % n_seq},
        )

    for shift in range(1, n_seq):
        share(shift).start()
    down_out.start()
    for i in range(SLABS):
        slab_in(i).wait()

        @pl.loop(0, slab // 256)
        def _(j):
            at = pl.ds(pl.multiple_of(i * slab + j * 256, 256), 256)
            wgu[0, :, at] = jnp.swapaxes(wraw[at], 0, 1)

        slab_out(i).start()

    idt = idt_ref[...]
    top_count = idt.shape[0]
    kinds_t = lax.broadcasted_iota(jnp.int32, (experts, rows), 0)
    hot_t = [(idt[k : k + 1, :] == kinds_t).astype(F32) for k in range(top_count)]
    down = lax.broadcasted_iota(jnp.int32, (rows, rows), 0)
    along = lax.broadcasted_iota(jnp.int32, (rows, rows), 1)
    before_t = jnp.dot(
        sum(hot_t).astype(BF16), (down < along).astype(F32).astype(BF16), preferred_element_type=F32
    )
    meta[...] = jnp.zeros_like(meta)
    for k in range(top_count):
        slot_t = jnp.sum(before_t * hot_t[k], axis=0, keepdims=True)
        meta[k : k + 1, :] = idt[k : k + 1, :].astype(F32) * float(cap) + slot_t

    for shift in range(1, n_seq):
        share(shift).wait_recv()

    def lend(offset):
        return remote(
            picked.at[offset], sib.at[offset], ssend.at[offset], srecv.at[offset],
            {"branch": (branch + offset + 1) % n_branch},
        )

    upper = branch // 2
    for target in (2 - upper, near, 3 - 3 * upper):
        offset = (target - branch + n_branch - 1) % n_branch
        picked[offset] = own[(seq - list_ref[offset] + n_seq) % n_seq]
        lend(offset).start()

    def chunk(r):
        return pl.ds(pl.multiple_of(r * span, span), span)

    def columns(head, half):
        base = (head * group + half * pack) * HEAD_SIZE
        return [slice(base + i * HEAD_SIZE, base + (i + 1) * HEAD_SIZE) for i in range(pack)]

    def kv_cols(head):
        return (
            slice(head * HEAD_SIZE, (head + 1) * HEAD_SIZE),
            slice((kv_heads + head) * HEAD_SIZE, (kv_heads + head + 1) * HEAD_SIZE),
        )

    tall = pack * span

    @pl.loop(0, CHUNKS)
    def _(r):
        at_row = r * span + lax.broadcasted_iota(jnp.int32, (tall, own_len), 0) % span
        at_col = lax.broadcasted_iota(jnp.int32, (tall, own_len), 1)
        earlier = at_col // rows
        bias = jnp.where(
            earlier == 0,
            jnp.where(at_col <= at_row, 0.0, -1e30),
            jnp.where(earlier <= seq, 0.0, -1e30),
        )
        for head in range(kv_heads):
            kcol, vcol = kv_cols(head)
            for half in range(halves):
                cols = columns(head, half)
                q = jnp.concatenate([q_ref[chunk(r), c] for c in cols], axis=0)
                keys = own[:, :, kcol].reshape(own_len, HEAD_SIZE)
                values = own[:, :, vcol].reshape(own_len, HEAD_SIZE)
                scores = lax.dot_general(q, keys, nt, preferred_element_type=F32) * scale + bias
                top = jnp.max(scores, axis=1, keepdims=True)
                p = jnp.exp(scores - top)
                tops[r, head * halves + half] = top
                totals[r, head * halves + half] = jnp.sum(p, axis=1, keepdims=True)
                mixed = jnp.dot(p.astype(BF16), values, preferred_element_type=F32)
                for i, c in enumerate(cols):
                    state[chunk(r), c] = mixed[i * span : (i + 1) * span]

    for offset in range(n_branch - 1):
        lend(offset).wait_recv()

    def rows_out(r):
        return remote(
            norm.at[chunk(r)], raw.at[inner, chunk(r)], rowsend.at[r], rowrecv.at[inner, r],
            {"branch": onward},
        )

    @pl.loop(0, CHUNKS)
    def _(r):
        for head in range(kv_heads):
            kcol, vcol = kv_cols(head)
            for half in range(halves):
                cols = columns(head, half)
                q = jnp.concatenate([q_ref[chunk(r), c] for c in cols], axis=0)
                keys = sib[:, :, kcol].reshape(sib_len, HEAD_SIZE)
                values = sib[:, :, vcol].reshape(sib_len, HEAD_SIZE)
                scores = lax.dot_general(q, keys, nt, preferred_element_type=F32) * scale
                own_top = tops[r, head * halves + half]
                top = jnp.maximum(own_top, jnp.max(scores, axis=1, keepdims=True))
                p = jnp.exp(scores - top)
                shrink = jnp.exp(own_top - top)
                total = totals[r, head * halves + half] * shrink + jnp.sum(p, axis=1, keepdims=True)
                mixed = jnp.dot(p.astype(BF16), values, preferred_element_type=F32)
                inverse = 1.0 / total
                for i, c in enumerate(cols):
                    at = slice(i * span, (i + 1) * span)
                    context = (state[chunk(r), c] * shrink[at] + mixed[at]) * inverse[at]
                    state[chunk(r), c] = res_ref[chunk(r), c].astype(F32) + context.astype(BF16).astype(F32)
        full = state[chunk(r), :]
        norm[chunk(r), :] = (
            full * lax.rsqrt(jnp.mean(full * full, axis=1, keepdims=True) + 1e-06)
        ).astype(BF16)
        rows_out(r).start()

    logits_t = lax.dot_general(router_ref[...], norm[...], nt, preferred_element_type=F32)
    chosen_t = [jnp.sum(logits_t * hot_t[k], axis=0, keepdims=True) for k in range(top_count)]
    for k in range(top_count):
        meta[top_count + k : top_count + k + 1, :] = 1.0 / sum(
            jnp.exp(c - chosen_t[k]) for c in chosen_t
        )

    def meta_out():
        return remote(meta, xmeta.at[inner], msend.at[0], mrecv.at[inner], {"branch": onward})

    meta_out().start()

    early = CHUNKS // 2
    late = slice(early * span, rows)

    def relay(c):
        return remote(
            raw.at[0, late, part(c)], raw.at[2, late, part(c)], relsend.at[c], relrecv.at[c],
            {"branch": far},
        )

    def relay_rows(r):
        at = slice(r * span, (r + 1) * span)
        return remote(
            raw.at[0, at], raw.at[2, at], relsend.at[PARTS + r], relrecv.at[PARTS + r],
            {"branch": far},
        )

    def meta_relay():
        return remote(xmeta.at[0], xmeta.at[2], msend.at[1], mrecv.at[2], {"branch": far})

    def meta_of(g):
        return meta[...] if g == 0 else xmeta[g - 1]

    def slots_of(g, count):
        where = lax.broadcasted_iota(jnp.int32, (cap, rows), 0).astype(F32)
        given = meta_of(g)
        return given, [where + (holders[f] * cap).astype(F32) for f in range(count)]

    def picks(g, count):
        given, where = slots_of(g, count)
        return jnp.concatenate(
            [(given[0:1] == w).astype(F32) + (given[1:2] == w).astype(F32) for w in where], axis=0
        ).astype(BF16)

    def shares(g, count):
        given, where = slots_of(g, count)
        weight = jnp.concatenate(
            [
                jnp.where(given[0:1] == w, given[2:3], 0.0) + jnp.where(given[1:2] == w, given[3:4], 0.0)
                for w in where
            ],
            axis=0,
        ).T
        high = weight.astype(BF16)
        return high, (weight - high.astype(F32)).astype(BF16)

    def spot(g, f):
        if f == 1:
            return g, 1
        return (1 if g == 0 else g), f - 2

    def forward(g, f, c):
        tg, th = spot(g, f)
        return remote(
            fwd.at[g, f - 1, :, part(c)], recv.at[tg, th, :, part(c)],
            fsend.at[g, f - 1], drecv.at[tg, th], places[f],
        )

    def give(g, count, pick, c):
        source = norm[:, part(c)] if g == 0 else raw[g - 1, :, part(c)]
        taken = jnp.dot(pick, source, preferred_element_type=F32).astype(BF16)
        recv[g, 0, :, part(c)] = taken[:cap]
        for f in range(1, count):
            fwd[g, f - 1, :, part(c)] = taken[f * cap : (f + 1) * cap]
        for f in (3, 2, 1):
            if f < count and (g, f) != (2, 2):
                forward(g, f, c).start()

    def give_all(g, count):
        pick = picks(g, count)
        for c in range(PARTS):
            give(g, count, pick, c)

    def whole(g, h):
        return remote(recv.at[g, h], recv.at[g, h], fsend.at[0, 0], drecv.at[g, h], places[1])

    def back_to(g, c):
        return remote(
            res.at[g, 1, :, part(c)], back.at[g, 0, :, part(c)],
            bsend.at[g, 1], brecv.at[g, 0, c], places[1],
        )

    def down_line(g, c):
        slot = g // 2 * g
        return remote(
            res.at[g, 0, :, part(c)], back.at[slot, 1, :, part(c)],
            bsend.at[g, 0], brecv.at[slot, 1, c], places[2],
        )

    def pass_on(g, c):
        slot = g // 2 * g
        return remote(
            back.at[g, 0, :, part(c)], back.at[slot, 2, :, part(c)],
            lsend.at[g - 1], brecv.at[slot, 2, c], places[2],
        )

    def compute(g, first=False, quiet=False):
        whole(g, 1).wait_recv()
        if not first:
            pl.when(inner == 0)(lambda: whole(g, 0).wait_recv())
        x = recv[g].reshape(2 * cap, width)
        acts = []
        for h in range(2):
            gate = jnp.dot(x, wgu[h, 0], preferred_element_type=F32)
            up = jnp.dot(x, wgu[h, 1], preferred_element_type=F32)
            acts.append((gate / (1.0 + jnp.exp(-gate)) * up).astype(BF16))
        for c in range(PARTS):
            total = jnp.dot(acts[0], wdn[0, :, part(c)], preferred_element_type=F32)
            total += jnp.dot(acts[1], wdn[1, :, part(c)], preferred_element_type=F32)
            res[g, :, :, part(c)] = total.astype(BF16).reshape(2, cap, step)
            if not quiet:
                back_to(g, c).start()

    def compute_half(g, h, opening):
        if opening:
            pl.when(inner == 0)(lambda: whole(g, h).wait_recv())
        else:
            whole(g, h).wait_recv()
        x = recv[g, h]
        acts = []
        for i in range(2):
            gate = jnp.dot(x, wgu[i, 0], preferred_element_type=F32)
            up = jnp.dot(x, wgu[i, 1], preferred_element_type=F32)
            acts.append((gate / (1.0 + jnp.exp(-gate)) * up).astype(BF16))
        for c in range(PARTS):
            total = jnp.dot(acts[0], wdn[0, :, part(c)], preferred_element_type=F32)
            total += jnp.dot(acts[1], wdn[1, :, part(c)], preferred_element_type=F32)
            res[g, h, :, part(c)] = total.astype(BF16)
            pl.when(inner == 1 - opening)(lambda: back_to(g, c).start())
            if not opening and c < PARTS // 2:
                pl.when(inner == 0)(lambda: down_line(g, c).start())

    def start_all(copy, g):
        for c in range(PARTS):
            copy(g, c).start()

    def pass_part(g, c):
        back_to(g, c).wait_recv()
        pass_on(g, c).start()

    def pass_all(g, first, ahead):
        for c in range(first, PARTS):
            pass_part(g, c)
            if ahead and c - first + ahead < PARTS:
                down_line(g, c - first + ahead).start()

    def combined(g, count, weight, c):
        for f in range(count - 1):
            remote(
                back.at[g, f, :, part(c)], back.at[g, f, :, part(c)],
                bsend.at[0, 0], brecv.at[g, f, c], places[1],
            ).wait_recv()
        given = jnp.concatenate(
            [res[g, 0, :, part(c)]] + [back[g, f, :, part(c)] for f in range(count - 1)], axis=0
        )
        return jnp.dot(weight[0], given, preferred_element_type=F32) + jnp.dot(
            weight[1], given, preferred_element_type=F32
        )

    def result(s, c):
        if s == 2:
            return remote(xout.at[2, c], fin.at[0, c], osend.at[2, c], orecv.at[0, c], {"branch": near})
        return remote(xout.at[s, c], fin.at[s, c], osend.at[s, c], orecv.at[s, c], {"branch": far})

    def wait_meta(g):
        remote(xmeta.at[g - 1], xmeta.at[g - 1], msend.at[0], mrecv.at[g - 1], places[2]).wait_recv()

    def wait_chunks(g, chunks):
        for r in chunks:
            at = slice(r * span, (r + 1) * span)
            remote(
                raw.at[g - 1, at], raw.at[g - 1, at], rowsend.at[0], rowrecv.at[g - 1, r], places[2]
            ).wait_recv()

    is_inner = pl.when(inner == 1)
    is_outer = pl.when(inner == 0)

    is_inner(lambda: give_all(0, 4))
    is_outer(lambda: give_all(0, 2))

    for i in range(SLABS):
        slab_out(i).wait_recv()
    down_out.wait_recv()
    down_in.wait()


    def far_rows(c, pick):
        relay(c).wait_recv()
        give(3, 4, pick, c)

    @is_inner
    def _():
        wait_chunks(1, range(early))
        for r in range(early):
            relay_rows(r).start()
        compute(0, True)
        wait_chunks(1, range(early, CHUNKS))
        wait_meta(1)
        meta_relay().start()
        for c in range(PARTS):
            relay(c).start()
        wait_chunks(2, range(CHUNKS))
        wait_meta(2)
        give_all(2, 4)
        for c in range(PARTS):
            forward(2, 2, c).start()
        wait_meta(3)
        for r in range(early):
            relay_rows(r).wait_recv()
        far_rows(0, picks(3, 4))

    compute(1 + inner, quiet=True)
    is_inner(lambda: start_all(back_to, 2))
    is_outer(lambda: start_all(down_line, 1))

    def send_far(s, weight, c):
        xout[s, c] = combined(2 + s, 4, weight, c).astype(BF16)
        result(s, c).start()

    def settle(count):
        weight = shares(0, count)
        for c in range(PARTS):
            state[:, part(c)] += combined(0, count, weight, c)

    @is_inner
    def _():
        pick = picks(3, 4)
        for c in range(1, PARTS):
            far_rows(c, pick)
        give_all(1, 2)

    lead = PARTS // 4
    compute_half(2 + inner, 1 - inner, 1)

    @is_outer
    def _():
        for c in range(lead):
            pass_part(2, c)

    @is_inner
    def _():
        weight = shares(2, 4)
        for c in range(PARTS // 2):
            send_far(0, weight, c)

    compute_half(2 + inner, inner, 0)
    is_outer(lambda: pass_all(2, lead, 2 * lead))

    @is_inner
    def _():
        weight = shares(2, 4)
        for c in range(PARTS // 2, PARTS):
            send_far(0, weight, c)

    compute(3 - 2 * inner)

    def arrived(s, c):
        remote(fin.at[s, c], fin.at[s, c], osend.at[0, 0], orecv.at[s, c], places[2]).wait_recv()

    def send_near(weight, c):
        partial = combined(1, 2, weight, c)
        arrived(1, c)
        xout[2, c] = (partial + fin[1, c].astype(F32)).astype(BF16)
        result(2, c).start()

    @is_inner
    def _():
        near_weight = shares(1, 2)
        weight = shares(3, 4)
        lag = PARTS // 2
        for c in range(PARTS):
            send_far(1, weight, c)
            if c >= lag:
                send_near(near_weight, c - lag)
        for c in range(PARTS - lag, PARTS):
            send_near(near_weight, c)
        settle(4)

    @is_outer
    def _():
        for c in range(lead):
            down_line(3, c).start()
        pass_all(3, 0, lead)
        start_all(back_to, 1)
        compute(0, True)
        pass_all(1, 0, 0)
        settle(2)

    def write(c):
        return pltpu.make_async_copy(done.at[:, part(c)], out_ref.at[:, part(c)], dsend.at[c])

    for c in range(PARTS):
        arrived(0, c)
        done[:, part(c)] = (state[:, part(c)] + fin[0, c].astype(F32)).astype(BF16)
        write(c).start()

    for c in range(PARTS):
        write(c).wait()
    for shift in range(1, n_seq):
        share(shift).wait_send()
    for i in range(SLABS):
        slab_out(i).wait_send()
    down_out.wait_send()
    for offset in range(n_branch - 1):
        lend(offset).wait_send()
    for r in range(CHUNKS):
        rows_out(r).wait_send()
    meta_out().wait_send()

    def sent(g, f):
        remote(fwd.at[g, f - 1], fwd.at[g, f - 1], fsend.at[g, f - 1], drecv.at[0, 0], places[1]).wait_send()

    def returned(g, h):
        remote(res.at[g, h], res.at[g, h], bsend.at[g, h], brecv.at[0, 0, 0], places[1]).wait_send()

    sent(0, 1)
    for g in range(4):
        returned(g, 1)

    @is_inner
    def _():
        for g in (0, 2, 3):
            for f in ((2, 3) if g == 0 else (1, 2, 3)):
                sent(g, f)
        sent(1, 1)
        for c in range(PARTS):
            relay(c).wait_send()
            if c < early:
                relay_rows(c).wait_send()
            for s in range(3):
                result(s, c).wait_send()
        meta_relay().wait_send()

    @is_outer
    def _():
        for g in (1, 2, 3):
            returned(g, 0)
            remote(back.at[g, 0], back.at[g, 0], lsend.at[g - 1], brecv.at[0, 0, 0], places[2]).wait_send()


def run_line(listed, q, kv, residual, router_t, idt, wgu, wdn, experts, cap, n_branch, n_seq):
    rows, width = q.shape
    ff = wdn.shape[0]
    kv_width = kv.shape[1] * kv.shape[2]
    part = width // PARTS
    tall = 2 * rows
    steps = width // HEAD_SIZE * rows // tall // CHUNKS
    dma = pltpu.SemaphoreType.DMA
    return pl.pallas_call(
        functools.partial(line_kernel, experts, cap, n_branch, n_seq),
        out_shape=jax.ShapeDtypeStruct((rows, width), BF16),
        in_specs=[SMEM] + [VMEM] * 5 + [ANY, ANY],
        out_specs=ANY,
        scratch_shapes=[
            pltpu.VMEM((n_seq, rows, kv_width), BF16),
            pltpu.VMEM((n_branch - 1, rows, kv_width), BF16),
            pltpu.VMEM((n_branch - 1, rows, kv_width), BF16),
            pltpu.VMEM((CHUNKS, steps, tall, 1), F32),
            pltpu.VMEM((CHUNKS, steps, tall, 1), F32),
            pltpu.VMEM((rows, width), F32),
            pltpu.VMEM((rows, width), BF16),
            pltpu.VMEM((3, rows, width), BF16),
            pltpu.VMEM((8, rows), F32),
            pltpu.VMEM((3, 8, rows), F32),
            pltpu.VMEM((4, 2, cap, width), BF16),
            pltpu.VMEM((4, 2, cap, width), BF16),
            pltpu.VMEM((4, 3, cap, width), BF16),
            pltpu.VMEM((4, 3, cap, width), BF16),
            pltpu.VMEM((width, 2, ff), BF16),
            pltpu.VMEM((2, 2, width, ff), BF16),
            pltpu.VMEM((2, ff, width), BF16),
            pltpu.VMEM((3, PARTS, rows, part), BF16),
            pltpu.VMEM((2, PARTS, rows, part), BF16),
            pltpu.VMEM((rows, width), BF16),
            dma((n_seq - 1,)), dma((n_seq - 1,)), dma((n_branch - 1,)), dma((n_branch - 1,)),
            dma((SLABS + 1,)), dma((SLABS + 1,)), dma((SLABS + 1,)),
            dma((CHUNKS,)), dma((2, CHUNKS)), dma((PARTS + CHUNKS // 2,)), dma((PARTS + CHUNKS // 2,)), dma((2,)), dma((3,)),
            dma((4, 3)), dma((4, 2)), dma((4, 2)), dma((4, 3, PARTS)), dma((3,)), dma((3, PARTS)), dma((2, PARTS)), dma((PARTS,)),
        ],
        compiler_params=pltpu.CompilerParams(
            collective_id=2, has_side_effects=True, vmem_limit_bytes=LINE_VMEM_LIMIT
        ),
    )(listed, q, kv, residual, router_t, idt, wgu, wdn)


def on_device(
    n_branch, n_seq, queries, keyvals, residual, read_list, router, expert_ids, w_gate_up, w_down
):
    rows = queries.shape[1]
    experts = router.shape[1]
    top_count = expert_ids.shape[2]
    capacity = 2 * ((3 * rows * top_count + 4 * experts - 1) // (4 * experts))
    cap = (capacity + 15) // 16 * 16
    if n_branch == 4 and n_seq == 4 and experts == 8 and top_count == 2:
        return run_line(
            read_list.reshape(-1), queries[0], keyvals[0], residual[0], router.T, expert_ids[0].T,
            w_gate_up[0], w_down[0], experts, cap, n_branch, n_seq,
        )[None]
    kv = keyvals.reshape(rows, -1)
    wgu = jnp.swapaxes(w_gate_up[0], 0, 1)
    shifts = [
        lax.ppermute(kv, "seq", [(i, (i + step) % n_seq) for i in range(n_seq)])
        for step in range(1, n_seq)
    ]
    own = jnp.stack([kv] + shifts)
    send, state, gate, normed, meta = attend(
        read_list.reshape(-1), queries[0], own, residual[0], router.T, expert_ids[0],
        experts, experts, cap, n_branch, n_seq,
    )
    return run_experts(send, state, gate, wgu, w_down[0], experts, cap, n_seq)[None]


def solution(mesh):
    return jax.shard_map(
        functools.partial(on_device, mesh.shape["branch"], mesh.shape["seq"]),
        mesh=mesh,
        in_specs=(
            P(("rollout", "branch"), "seq", None),
            P(("rollout", "branch"), "seq", None, None),
            P(("rollout", "branch"), "seq", None),
            P(("rollout", "branch"), "seq", None),
            P(),
            P(("rollout", "branch"), "seq", None),
            P(("branch", "seq"), None, None, None),
            P(("branch", "seq"), None, None),
        ),
        out_specs=P(("rollout", "branch"), "seq", None),
        check_vma=False,
    )
```

```python
import functools
import math

import jax
import jax.numpy as jnp
from jax import lax
from jax.experimental import pallas as pl
from jax.experimental.pallas import tpu as pltpu
from jax.sharding import PartitionSpec as P

HEAD_SIZE = 128
PARTS = 8
CHUNKS = 8
SLABS = 4
VMEM_LIMIT = 60 * 1024 * 1024
LINE_VMEM_LIMIT = 63 * 1024 * 1024
F32 = jnp.float32
BF16 = jnp.bfloat16
ANY = pl.BlockSpec(memory_space=pl.ANY)
VMEM = pl.BlockSpec(memory_space=pltpu.VMEM)
SMEM = pl.BlockSpec(memory_space=pltpu.SMEM)


def flipped(number, mask, count):
    value, bit = 0, 1
    while bit < count:
        value = value + ((number // bit + mask // bit) % 2) * bit
        bit *= 2
    return value


def attend_kernel(
    experts, cap, n_branch, n_seq,
    list_ref, q_ref, own_ref, res_ref, router_ref, ids_ref, idt_ref,
    send_ref, state_ref, gate_ref, norm_ref, meta_ref,
    picked, sib_ref, tops, totals, ssem, rsem,
):
    branch = lax.axis_index("branch")
    seq = lax.axis_index("seq")
    me = (branch * n_seq + seq) // 2
    rows, width = q_ref.shape
    kv_heads = own_ref.shape[2] // (2 * HEAD_SIZE)
    group = width // HEAD_SIZE // kv_heads
    together = 2
    tall = together * rows
    own_len = n_seq * rows
    sib_len = (n_branch - 1) * rows
    scale = 1.0 / math.sqrt(HEAD_SIZE)
    nt = (((1,), (1,)), ((), ()))

    barrier = pltpu.get_barrier_semaphore()
    for step in range(1, n_branch):
        pl.semaphore_signal(
            barrier, inc=1, device_id={"branch": (branch + step) % n_branch},
            device_id_type=pl.DeviceIdType.MESH,
        )
    for offset in range(n_branch - 1):
        picked[offset] = own_ref[(seq - list_ref[offset] + n_seq) % n_seq]
    pl.semaphore_wait(barrier, n_branch - 1)
    copies = []
    for offset in range(n_branch - 1):
        copy = pltpu.make_async_remote_copy(
            src_ref=picked.at[offset], dst_ref=sib_ref.at[offset],
            send_sem=ssem.at[offset], recv_sem=rsem.at[offset],
            device_id={"branch": (branch + offset + 1) % n_branch},
            device_id_type=pl.DeviceIdType.MESH,
        )
        copy.start()
        copies.append(copy)

    at_row = lax.broadcasted_iota(jnp.int32, (tall, own_len), 0) % rows
    at_col = lax.broadcasted_iota(jnp.int32, (tall, own_len), 1)
    earlier = at_col // rows
    bias = jnp.where(
        earlier == 0,
        jnp.where(at_col <= at_row, 0.0, -1e30),
        jnp.where(earlier <= seq, 0.0, -1e30),
    )

    def head_parts(head, step):
        base = (head * group + step * together) * HEAD_SIZE
        cols = [
            pl.ds(pl.multiple_of(base + i * HEAD_SIZE, HEAD_SIZE), HEAD_SIZE)
            for i in range(together)
        ]
        return cols, jnp.concatenate([q_ref[:, c] for c in cols], axis=0)

    def kv_cols(head):
        return (
            slice(head * HEAD_SIZE, (head + 1) * HEAD_SIZE),
            slice((kv_heads + head) * HEAD_SIZE, (kv_heads + head + 1) * HEAD_SIZE),
        )

    steps = group // together
    for head in range(kv_heads):
        kcol, vcol = kv_cols(head)

        @pl.loop(0, steps)
        def _(step):
            cols, q = head_parts(head, step)
            keys = own_ref[:, :, kcol].reshape(own_len, HEAD_SIZE)
            values = own_ref[:, :, vcol].reshape(own_len, HEAD_SIZE)
            scores = lax.dot_general(q, keys, nt, preferred_element_type=F32) * scale + bias
            top = jnp.max(scores, axis=1, keepdims=True)
            p = jnp.exp(scores - top)
            tops[head * steps + step] = top
            totals[head * steps + step] = jnp.sum(p, axis=1, keepdims=True)
            mixed = jnp.dot(p.astype(BF16), values, preferred_element_type=F32)
            for i, c in enumerate(cols):
                state_ref[:, c] = mixed[i * rows : (i + 1) * rows]

    for copy in copies:
        copy.wait()
    for head in range(kv_heads):
        kcol, vcol = kv_cols(head)

        @pl.loop(0, steps)
        def _(step):
            cols, q = head_parts(head, step)
            keys = sib_ref[:, :, kcol].reshape(sib_len, HEAD_SIZE)
            values = sib_ref[:, :, vcol].reshape(sib_len, HEAD_SIZE)
            scores = lax.dot_general(q, keys, nt, preferred_element_type=F32) * scale
            own_top = tops[head * steps + step]
            top = jnp.maximum(own_top, jnp.max(scores, axis=1, keepdims=True))
            p = jnp.exp(scores - top)
            shrink = jnp.exp(own_top - top)
            total = totals[head * steps + step] * shrink + jnp.sum(p, axis=1, keepdims=True)
            mixed = jnp.dot(p.astype(BF16), values, preferred_element_type=F32)
            inverse = 1.0 / total
            for i, c in enumerate(cols):
                part = slice(i * rows, (i + 1) * rows)
                context = (state_ref[:, c] * shrink[part] + mixed[part]) * inverse[part]
                state_ref[:, c] = res_ref[:, c].astype(F32) + context.astype(BF16).astype(F32)

    state = state_ref[...]
    normed = (
        state * lax.rsqrt(jnp.mean(state * state, axis=1, keepdims=True) + 1e-06)
    ).astype(BF16)
    logits = lax.dot_general(normed, router_ref[...], nt, preferred_element_type=F32)

    top_count = ids_ref.shape[1]
    ids, idt = ids_ref[...], idt_ref[...]
    kinds = lax.broadcasted_iota(jnp.int32, (rows, experts), 1)
    kinds_t = lax.broadcasted_iota(jnp.int32, (experts, rows), 0)
    hot = [(ids[:, k : k + 1] == kinds).astype(F32) for k in range(top_count)]
    hot_t = [(idt[k : k + 1, :] == kinds_t).astype(F32) for k in range(top_count)]
    down = lax.broadcasted_iota(jnp.int32, (rows, rows), 0)
    along = lax.broadcasted_iota(jnp.int32, (rows, rows), 1)
    before = jnp.dot((along < down).astype(F32).astype(BF16), sum(hot).astype(BF16), preferred_element_type=F32)
    before_t = jnp.dot(sum(hot_t).astype(BF16), (down < along).astype(F32).astype(BF16), preferred_element_type=F32)
    dest, dest_t = [], []
    for k in range(top_count):
        slot = jnp.sum(before * hot[k], axis=1, keepdims=True).astype(jnp.int32)
        dest.append((ids[:, k : k + 1] ^ me) * cap + slot)
        slot_t = jnp.sum(before_t * hot_t[k], axis=0, keepdims=True).astype(jnp.int32)
        dest_t.append((idt[k : k + 1, :] ^ me) * cap + slot_t)
    chosen = [jnp.sum(logits * hot[k], axis=1, keepdims=True) for k in range(top_count)]
    gates = [1.0 / sum(jnp.exp(c - chosen[k]) for c in chosen) for k in range(top_count)]

    parts, _, part_width = norm_ref.shape
    for c in range(parts):
        norm_ref[c] = normed[:, c * part_width : (c + 1) * part_width]
    logits_t = lax.dot_general(router_ref[...], normed, nt, preferred_element_type=F32)
    chosen_t = [jnp.sum(logits_t * hot_t[k], axis=0, keepdims=True) for k in range(top_count)]
    meta_ref[...] = jnp.zeros_like(meta_ref)
    for k in range(top_count):
        meta_ref[k : k + 1, :] = dest_t[k].astype(F32)
        meta_ref[top_count + k : top_count + k + 1, :] = 1.0 / sum(
            jnp.exp(c - chosen_t[k]) for c in chosen_t
        )

    pair = 2 * cap
    places = lax.broadcasted_iota(jnp.int32, (rows, pair), 1)
    places_t = lax.broadcasted_iota(jnp.int32, (pair, rows), 0)
    for p in range(send_ref.shape[0] // pair):
        pick = sum((dest_t[k] - p * pair == places_t).astype(F32) for k in range(top_count))
        send_ref[p * pair : (p + 1) * pair, :] = jnp.dot(
            pick.astype(BF16), normed, preferred_element_type=F32
        ).astype(BF16)
        weight = sum(
            jnp.where(dest[k] - p * pair == places, gates[k], 0.0) for k in range(top_count)
        )
        high = weight.astype(BF16)
        gate_ref[p, 0] = high
        gate_ref[p, 1] = (weight - high.astype(F32)).astype(BF16)


def attend(listed, q, own, residual, router_t, ids, experts, near, cap, n_branch, n_seq):
    rows, width = q.shape
    halves = width // HEAD_SIZE // 2
    return pl.pallas_call(
        functools.partial(attend_kernel, experts, cap, n_branch, n_seq),
        out_shape=(
            jax.ShapeDtypeStruct((near * cap, width), BF16),
            jax.ShapeDtypeStruct((rows, width), F32),
            jax.ShapeDtypeStruct((near // 2, 2, rows, 2 * cap), BF16),
            jax.ShapeDtypeStruct((PARTS, rows, width // PARTS), BF16),
            jax.ShapeDtypeStruct((8, rows), F32),
        ),
        in_specs=[SMEM] + [VMEM] * 6,
        out_specs=(VMEM,) * 5,
        scratch_shapes=[
            pltpu.VMEM((n_branch - 1, rows, own.shape[2]), BF16),
            pltpu.VMEM((n_branch - 1, rows, own.shape[2]), BF16),
            pltpu.VMEM((halves, 2 * rows, 1), F32),
            pltpu.VMEM((halves, 2 * rows, 1), F32),
            pltpu.SemaphoreType.DMA((n_branch,)),
            pltpu.SemaphoreType.DMA((n_branch,)),
        ],
        compiler_params=pltpu.CompilerParams(
            collective_id=0, has_side_effects=True, vmem_limit_bytes=VMEM_LIMIT
        ),
    )(listed, q, own, residual, router_t, ids, ids.T)


def expert_kernel(
    experts, cap, n_seq,
    send_ref, state_ref, gate_ref, wgu_ref, wdn_ref, out_ref,
    recv, res, ret, wgu, wdn, acc,
    wsend, wrecv, wloc, lsem, dsend, drecv, bsend, brecv,
):
    branch = lax.axis_index("branch")
    seq = lax.axis_index("seq")
    core = seq % 2
    me = (branch * n_seq + seq) // 2
    pair = 2 * cap
    width = send_ref.shape[1]
    twin = {"seq": seq + 1 - 2 * core}
    mesh_id = pl.DeviceIdType.MESH

    def place(k):
        other = flipped(me, k, experts)
        return {"branch": (2 * other) // n_seq, "seq": (2 * other) % n_seq + core}

    barrier = pltpu.get_barrier_semaphore()
    pl.semaphore_signal(barrier, inc=1, device_id=twin, device_id_type=mesh_id)

    @pl.loop(1, experts)
    def _(k):
        pl.semaphore_signal(barrier, inc=1, device_id=place(k), device_id_type=mesh_id)

    pl.semaphore_wait(barrier, experts)

    def block(k):
        return pl.ds(pl.multiple_of(k * cap, 16), cap)

    def dispatch(k):
        return pltpu.make_async_remote_copy(
            src_ref=send_ref.at[block(k)], dst_ref=recv.at[block(k)],
            send_sem=dsend.at[k], recv_sem=drecv.at[k],
            device_id=place(k), device_id_type=mesh_id,
        )

    def give_back(k):
        return pltpu.make_async_remote_copy(
            src_ref=res.at[block(k)], dst_ref=ret.at[block(k)],
            send_sem=bsend.at[k], recv_sem=brecv.at[k],
            device_id=place(k), device_id_type=mesh_id,
        )

    weights = []
    for i, (src, dst) in enumerate(((wgu_ref, wgu), (wdn_ref, wdn))):
        weights.append(
            pltpu.make_async_remote_copy(
                src_ref=src, dst_ref=dst.at[1], send_sem=wsend.at[i], recv_sem=wrecv.at[i],
                device_id=twin, device_id_type=mesh_id,
            )
        )
        weights.append(pltpu.make_async_copy(src, dst.at[0], wloc.at[i]))
    dispatch(1).start()
    mine = pltpu.make_async_copy(send_ref.at[block(0)], recv.at[block(0)], lsem)
    mine.start()

    @pl.loop(experts // 2, experts)
    def _(k):
        dispatch(k).start()

    @pl.loop(2, experts // 2)
    def _(k):
        dispatch(k).start()

    for copy in weights:
        copy.start()
    acc[...] = state_ref[...]
    for copy in weights:
        copy.wait()

    chunk = 512

    def compute(p):
        span = pl.ds(pl.multiple_of(p * pair, 16), pair)
        acts = []
        for h in range(2):
            x = recv[span, :]
            gate = jnp.dot(x, wgu[h, 0], preferred_element_type=F32)
            up = jnp.dot(x, wgu[h, 1], preferred_element_type=F32)
            acts.append((gate / (1.0 + jnp.exp(-gate)) * up).astype(BF16))
        for start in range(0, width, chunk):
            cols = slice(start, start + chunk)
            done = jnp.dot(acts[0], wdn[0, :, cols], preferred_element_type=F32)
            done += jnp.dot(acts[1], wdn[1, :, cols], preferred_element_type=F32)
            res[span, cols] = done.astype(BF16)

    quarter = experts // 4

    def turn(i):
        return jnp.where(i <= quarter, i + quarter - 1, i - quarter)

    mine.wait()
    dispatch(1).wait_recv()
    compute(0)
    give_back(1).start()

    @pl.loop(1, experts // 2)
    def _(i):
        p = turn(i)
        dispatch(2 * p).wait_recv()
        dispatch(2 * p + 1).wait_recv()
        compute(p)
        give_back(2 * p).start()
        give_back(2 * p + 1).start()

    def add(p, rows):
        for start in range(0, width, chunk):
            cols = slice(start, start + chunk)
            block_rows = rows(cols)
            acc[:, cols] += jnp.dot(
                gate_ref[p, 0], block_rows, preferred_element_type=F32
            ) + jnp.dot(gate_ref[p, 1], block_rows, preferred_element_type=F32)

    give_back(1).wait_recv()
    add(0, lambda cols: jnp.concatenate([res[0:cap, cols], ret[cap:pair, cols]], axis=0))

    @pl.loop(1, experts // 2)
    def _(i):
        p = turn(i)
        give_back(2 * p).wait_recv()
        give_back(2 * p + 1).wait_recv()
        span = pl.ds(pl.multiple_of(p * pair, 16), pair)
        add(p, lambda cols: ret[span, cols])

    out_ref[...] = acc[...].astype(BF16)

    @pl.loop(1, experts)
    def _(k):
        dispatch(k).wait_send()
        give_back(k).wait_send()


def run_experts(send, state, gate, wgu, wdn, experts, cap, n_seq):
    rows, width = state.shape
    ff = wdn.shape[0]
    return pl.pallas_call(
        functools.partial(expert_kernel, experts, cap, n_seq),
        out_shape=jax.ShapeDtypeStruct((rows, width), BF16),
        in_specs=[ANY, VMEM, VMEM, ANY, ANY],
        out_specs=VMEM,
        scratch_shapes=[
            pltpu.VMEM((experts * cap, width), BF16),
            pltpu.VMEM((experts * cap, width), BF16),
            pltpu.VMEM((experts * cap, width), BF16),
            pltpu.VMEM((2, 2, width, ff), BF16),
            pltpu.VMEM((2, ff, width), BF16),
            pltpu.VMEM((rows, width), F32),
            pltpu.SemaphoreType.DMA((2,)),
            pltpu.SemaphoreType.DMA((2,)),
            pltpu.SemaphoreType.DMA((2,)),
            pltpu.SemaphoreType.DMA,
            pltpu.SemaphoreType.DMA((experts,)),
            pltpu.SemaphoreType.DMA((experts,)),
            pltpu.SemaphoreType.DMA((experts,)),
            pltpu.SemaphoreType.DMA((experts,)),
        ],
        compiler_params=pltpu.CompilerParams(
            collective_id=1, has_side_effects=True, vmem_limit_bytes=VMEM_LIMIT
        ),
    )(send, state, gate, wgu, wdn)


def line_kernel(
    experts, cap, n_branch, n_seq,
    list_ref, q_ref, kv_ref, res_ref, router_ref, idt_ref, wgu_ref, wdn_ref,
    out_ref,
    own, picked, sib, tops, totals, state, norm, raw, meta, xmeta,
    recv, res, back, fwd, wraw, wgu, wdn, xout, fin, done,
    ksend, krecv, ssend, srecv, wsend, wrecv, wloc,
    rowsend, rowrecv, relsend, relrecv, msend, mrecv,
    fsend, drecv, bsend, brecv, lsend, osend, orecv, dsend,
):
    branch = lax.axis_index("branch")
    seq = lax.axis_index("seq")
    inner = (branch + 1) // 2 % 2
    mesh_id = pl.DeviceIdType.MESH
    rows, width = q_ref.shape
    kv_heads = own.shape[2] // (2 * HEAD_SIZE)
    group = width // HEAD_SIZE // kv_heads
    own_len = n_seq * rows
    sib_len = (n_branch - 1) * rows
    scale = 1.0 / math.sqrt(HEAD_SIZE)
    nt = (((1,), (1,)), ((), ()))
    step = width // PARTS
    span = rows // CHUNKS
    pack = 2 * rows // span
    halves = group // pack

    across = (seq + 2) % n_seq
    near = branch + 1 - 2 * (branch % 2)
    far = n_branch - 1 - branch
    onward = near + inner * (far - near)
    places = [
        {"branch": branch, "seq": seq},
        {"branch": branch, "seq": across},
        {"branch": near, "seq": seq},
        {"branch": near, "seq": across},
    ]
    holders = [(p["branch"] * n_seq + p["seq"]) // 2 for p in places]

    def remote(src, dst, send, arrive, device):
        return pltpu.make_async_remote_copy(
            src_ref=src, dst_ref=dst, send_sem=send, recv_sem=arrive,
            device_id=device, device_id_type=mesh_id,
        )

    def part(c):
        return slice(c * step, (c + 1) * step)

    twin = {"seq": seq + 1 - 2 * (seq % 2)}
    slab = width // SLABS

    def slab_in(i):
        at = slice(i * slab, (i + 1) * slab)
        return pltpu.make_async_copy(wgu_ref.at[at], wraw.at[at], wloc.at[i])

    def slab_out(i):
        at = slice(i * slab, (i + 1) * slab)
        return remote(wgu.at[0, :, at], wgu.at[1, :, at], wsend.at[i], wrecv.at[i], twin)

    down_in = pltpu.make_async_copy(wdn_ref, wdn.at[0], wloc.at[SLABS])
    down_out = remote(wdn_ref, wdn.at[1], wsend.at[SLABS], wrecv.at[SLABS], twin)
    for i in range(SLABS):
        slab_in(i).start()
    down_in.start()
    own[0] = kv_ref[...].reshape(rows, own.shape[2])

    barrier = pltpu.get_barrier_semaphore()
    for shift in range(1, n_branch):
        pl.semaphore_signal(
            barrier, inc=1, device_id={"branch": (branch + shift) % n_branch}, device_id_type=mesh_id
        )
    for shift in range(1, n_seq):
        pl.semaphore_signal(
            barrier, inc=1, device_id={"seq": (seq + shift) % n_seq}, device_id_type=mesh_id
        )
    pl.semaphore_wait(barrier, n_branch + n_seq - 2)

    def share(shift):
        return remote(
            own.at[0], own.at[shift], ksend.at[shift - 1], krecv.at[shift - 1],
            {"seq": (seq + shift) % n_seq},
        )

    for shift in range(1, n_seq):
        share(shift).start()
    down_out.start()
    for i in range(SLABS):
        slab_in(i).wait()

        @pl.loop(0, slab // 256)
        def _(j):
            at = pl.ds(pl.multiple_of(i * slab + j * 256, 256), 256)
            wgu[0, :, at] = jnp.swapaxes(wraw[at], 0, 1)

        slab_out(i).start()

    idt = idt_ref[...]
    top_count = idt.shape[0]
    kinds_t = lax.broadcasted_iota(jnp.int32, (experts, rows), 0)
    hot_t = [(idt[k : k + 1, :] == kinds_t).astype(F32) for k in range(top_count)]
    down = lax.broadcasted_iota(jnp.int32, (rows, rows), 0)
    along = lax.broadcasted_iota(jnp.int32, (rows, rows), 1)
    before_t = jnp.dot(
        sum(hot_t).astype(BF16), (down < along).astype(F32).astype(BF16), preferred_element_type=F32
    )
    meta[...] = jnp.zeros_like(meta)
    for k in range(top_count):
        slot_t = jnp.sum(before_t * hot_t[k], axis=0, keepdims=True)
        meta[k : k + 1, :] = idt[k : k + 1, :].astype(F32) * float(cap) + slot_t

    for shift in range(1, n_seq):
        share(shift).wait_recv()

    def lend(offset):
        return remote(
            picked.at[offset], sib.at[offset], ssend.at[offset], srecv.at[offset],
            {"branch": (branch + offset + 1) % n_branch},
        )

    upper = branch // 2
    for target in (2 - upper, near, 3 - 3 * upper):
        offset = (target - branch + n_branch - 1) % n_branch
        picked[offset] = own[(seq - list_ref[offset] + n_seq) % n_seq]
        lend(offset).start()

    def chunk(r):
        return pl.ds(pl.multiple_of(r * span, span), span)

    def columns(head, half):
        base = (head * group + half * pack) * HEAD_SIZE
        return [slice(base + i * HEAD_SIZE, base + (i + 1) * HEAD_SIZE) for i in range(pack)]

    def kv_cols(head):
        return (
            slice(head * HEAD_SIZE, (head + 1) * HEAD_SIZE),
            slice((kv_heads + head) * HEAD_SIZE, (kv_heads + head + 1) * HEAD_SIZE),
        )

    tall = pack * span

    @pl.loop(0, CHUNKS)
    def _(r):
        at_row = r * span + lax.broadcasted_iota(jnp.int32, (tall, own_len), 0) % span
        at_col = lax.broadcasted_iota(jnp.int32, (tall, own_len), 1)
        earlier = at_col // rows
        bias = jnp.where(
            earlier == 0,
            jnp.where(at_col <= at_row, 0.0, -1e30),
            jnp.where(earlier <= seq, 0.0, -1e30),
        )
        for head in range(kv_heads):
            kcol, vcol = kv_cols(head)
            for half in range(halves):
                cols = columns(head, half)
                q = jnp.concatenate([q_ref[chunk(r), c] for c in cols], axis=0)
                keys = own[:, :, kcol].reshape(own_len, HEAD_SIZE)
                values = own[:, :, vcol].reshape(own_len, HEAD_SIZE)
                scores = lax.dot_general(q, keys, nt, preferred_element_type=F32) * scale + bias
                top = jnp.max(scores, axis=1, keepdims=True)
                p = jnp.exp(scores - top)
                tops[r, head * halves + half] = top
                totals[r, head * halves + half] = jnp.sum(p, axis=1, keepdims=True)
                mixed = jnp.dot(p.astype(BF16), values, preferred_element_type=F32)
                for i, c in enumerate(cols):
                    state[chunk(r), c] = mixed[i * span : (i + 1) * span]

    for offset in range(n_branch - 1):
        lend(offset).wait_recv()

    def rows_out(r):
        return remote(
            norm.at[chunk(r)], raw.at[inner, chunk(r)], rowsend.at[r], rowrecv.at[inner, r],
            {"branch": onward},
        )

    @pl.loop(0, CHUNKS)
    def _(r):
        for head in range(kv_heads):
            kcol, vcol = kv_cols(head)
            for half in range(halves):
                cols = columns(head, half)
                q = jnp.concatenate([q_ref[chunk(r), c] for c in cols], axis=0)
                keys = sib[:, :, kcol].reshape(sib_len, HEAD_SIZE)
                values = sib[:, :, vcol].reshape(sib_len, HEAD_SIZE)
                scores = lax.dot_general(q, keys, nt, preferred_element_type=F32) * scale
                own_top = tops[r, head * halves + half]
                top = jnp.maximum(own_top, jnp.max(scores, axis=1, keepdims=True))
                p = jnp.exp(scores - top)
                shrink = jnp.exp(own_top - top)
                total = totals[r, head * halves + half] * shrink + jnp.sum(p, axis=1, keepdims=True)
                mixed = jnp.dot(p.astype(BF16), values, preferred_element_type=F32)
                inverse = 1.0 / total
                for i, c in enumerate(cols):
                    at = slice(i * span, (i + 1) * span)
                    context = (state[chunk(r), c] * shrink[at] + mixed[at]) * inverse[at]
                    state[chunk(r), c] = res_ref[chunk(r), c].astype(F32) + context.astype(BF16).astype(F32)
        full = state[chunk(r), :]
        norm[chunk(r), :] = (
            full * lax.rsqrt(jnp.mean(full * full, axis=1, keepdims=True) + 1e-06)
        ).astype(BF16)
        rows_out(r).start()

    logits_t = lax.dot_general(router_ref[...], norm[...], nt, preferred_element_type=F32)
    chosen_t = [jnp.sum(logits_t * hot_t[k], axis=0, keepdims=True) for k in range(top_count)]
    for k in range(top_count):
        meta[top_count + k : top_count + k + 1, :] = 1.0 / sum(
            jnp.exp(c - chosen_t[k]) for c in chosen_t
        )

    def meta_out():
        return remote(meta, xmeta.at[inner], msend.at[0], mrecv.at[inner], {"branch": onward})

    meta_out().start()

    early = CHUNKS // 2
    late = slice(early * span, rows)

    def relay(c):
        return remote(
            raw.at[0, late, part(c)], raw.at[2, late, part(c)], relsend.at[c], relrecv.at[c],
            {"branch": far},
        )

    def relay_rows(r):
        at = slice(r * span, (r + 1) * span)
        return remote(
            raw.at[0, at], raw.at[2, at], relsend.at[PARTS + r], relrecv.at[PARTS + r],
            {"branch": far},
        )

    def meta_relay():
        return remote(xmeta.at[0], xmeta.at[2], msend.at[1], mrecv.at[2], {"branch": far})

    def meta_of(g):
        return meta[...] if g == 0 else xmeta[g - 1]

    def slots_of(g, count):
        where = lax.broadcasted_iota(jnp.int32, (cap, rows), 0).astype(F32)
        given = meta_of(g)
        return given, [where + (holders[f] * cap).astype(F32) for f in range(count)]

    def picks(g, count):
        given, where = slots_of(g, count)
        return jnp.concatenate(
            [(given[0:1] == w).astype(F32) + (given[1:2] == w).astype(F32) for w in where], axis=0
        ).astype(BF16)

    def shares(g, count):
        given, where = slots_of(g, count)
        weight = jnp.concatenate(
            [
                jnp.where(given[0:1] == w, given[2:3], 0.0) + jnp.where(given[1:2] == w, given[3:4], 0.0)
                for w in where
            ],
            axis=0,
        ).T
        high = weight.astype(BF16)
        return high, (weight - high.astype(F32)).astype(BF16)

    def spot(g, f):
        if f == 1:
            return g, 1
        return (1 if g == 0 else g), f - 2

    def forward(g, f, c):
        tg, th = spot(g, f)
        return remote(
            fwd.at[g, f - 1, :, part(c)], recv.at[tg, th, :, part(c)],
            fsend.at[g, f - 1], drecv.at[tg, th], places[f],
        )

    def give(g, count, pick, c):
        source = norm[:, part(c)] if g == 0 else raw[g - 1, :, part(c)]
        taken = jnp.dot(pick, source, preferred_element_type=F32).astype(BF16)
        recv[g, 0, :, part(c)] = taken[:cap]
        for f in range(1, count):
            fwd[g, f - 1, :, part(c)] = taken[f * cap : (f + 1) * cap]
        for f in (3, 2, 1):
            if f < count and (g, f) != (2, 2):
                forward(g, f, c).start()

    def give_all(g, count):
        pick = picks(g, count)
        for c in range(PARTS):
            give(g, count, pick, c)

    def whole(g, h):
        return remote(recv.at[g, h], recv.at[g, h], fsend.at[0, 0], drecv.at[g, h], places[1])

    def back_to(g, c):
        return remote(
            res.at[g, 1, :, part(c)], back.at[g, 0, :, part(c)],
            bsend.at[g, 1], brecv.at[g, 0, c], places[1],
        )

    def down_line(g, c):
        slot = g // 2 * g
        return remote(
            res.at[g, 0, :, part(c)], back.at[slot, 1, :, part(c)],
            bsend.at[g, 0], brecv.at[slot, 1, c], places[2],
        )

    def pass_on(g, c):
        slot = g // 2 * g
        return remote(
            back.at[g, 0, :, part(c)], back.at[slot, 2, :, part(c)],
            lsend.at[g - 1], brecv.at[slot, 2, c], places[2],
        )

    def compute(g, first=False, quiet=False):
        whole(g, 1).wait_recv()
        if not first:
            pl.when(inner == 0)(lambda: whole(g, 0).wait_recv())
        x = recv[g].reshape(2 * cap, width)
        acts = []
        for h in range(2):
            gate = jnp.dot(x, wgu[h, 0], preferred_element_type=F32)
            up = jnp.dot(x, wgu[h, 1], preferred_element_type=F32)
            acts.append((gate / (1.0 + jnp.exp(-gate)) * up).astype(BF16))
        for c in range(PARTS):
            total = jnp.dot(acts[0], wdn[0, :, part(c)], preferred_element_type=F32)
            total += jnp.dot(acts[1], wdn[1, :, part(c)], preferred_element_type=F32)
            res[g, :, :, part(c)] = total.astype(BF16).reshape(2, cap, step)
            if not quiet:
                back_to(g, c).start()

    def compute_half(g, h, opening):
        if opening:
            pl.when(inner == 0)(lambda: whole(g, h).wait_recv())
        else:
            whole(g, h).wait_recv()
        x = recv[g, h]
        acts = []
        for i in range(2):
            gate = jnp.dot(x, wgu[i, 0], preferred_element_type=F32)
            up = jnp.dot(x, wgu[i, 1], preferred_element_type=F32)
            acts.append((gate / (1.0 + jnp.exp(-gate)) * up).astype(BF16))
        for c in range(PARTS):
            total = jnp.dot(acts[0], wdn[0, :, part(c)], preferred_element_type=F32)
            total += jnp.dot(acts[1], wdn[1, :, part(c)], preferred_element_type=F32)
            res[g, h, :, part(c)] = total.astype(BF16)
            pl.when(inner == 1 - opening)(lambda: back_to(g, c).start())
            if not opening and c < PARTS // 2:
                pl.when(inner == 0)(lambda: down_line(g, c).start())

    def start_all(copy, g):
        for c in range(PARTS):
            copy(g, c).start()

    def pass_part(g, c):
        back_to(g, c).wait_recv()
        pass_on(g, c).start()

    def pass_all(g, first, ahead):
        for c in range(first, PARTS):
            pass_part(g, c)
            if ahead and c - first + ahead < PARTS:
                down_line(g, c - first + ahead).start()

    def combined(g, count, weight, c):
        for f in range(count - 1):
            remote(
                back.at[g, f, :, part(c)], back.at[g, f, :, part(c)],
                bsend.at[0, 0], brecv.at[g, f, c], places[1],
            ).wait_recv()
        given = jnp.concatenate(
            [res[g, 0, :, part(c)]] + [back[g, f, :, part(c)] for f in range(count - 1)], axis=0
        )
        return jnp.dot(weight[0], given, preferred_element_type=F32) + jnp.dot(
            weight[1], given, preferred_element_type=F32
        )

    def result(s, c):
        if s == 2:
            return remote(xout.at[2, c], fin.at[0, c], osend.at[2, c], orecv.at[0, c], {"branch": near})
        return remote(xout.at[s, c], fin.at[s, c], osend.at[s, c], orecv.at[s, c], {"branch": far})

    def wait_meta(g):
        remote(xmeta.at[g - 1], xmeta.at[g - 1], msend.at[0], mrecv.at[g - 1], places[2]).wait_recv()

    def wait_chunks(g, chunks):
        for r in chunks:
            at = slice(r * span, (r + 1) * span)
            remote(
                raw.at[g - 1, at], raw.at[g - 1, at], rowsend.at[0], rowrecv.at[g - 1, r], places[2]
            ).wait_recv()

    is_inner = pl.when(inner == 1)
    is_outer = pl.when(inner == 0)

    is_inner(lambda: give_all(0, 4))
    is_outer(lambda: give_all(0, 2))

    for i in range(SLABS):
        slab_out(i).wait_recv()
    down_out.wait_recv()
    down_in.wait()


    def far_rows(c, pick):
        relay(c).wait_recv()
        give(3, 4, pick, c)

    @is_inner
    def _():
        wait_chunks(1, range(early))
        for r in range(early):
            relay_rows(r).start()
        compute(0, True)
        wait_chunks(2, range(CHUNKS))
        wait_meta(2)
        give_all(2, 4)
        for c in range(PARTS):
            forward(2, 2, c).start()
        wait_chunks(1, range(early, CHUNKS))
        wait_meta(1)
        meta_relay().start()
        for c in range(PARTS):
            relay(c).start()
        wait_meta(3)
        for r in range(early):
            relay_rows(r).wait_recv()
        far_rows(0, picks(3, 4))

    compute(1 + inner, quiet=True)
    is_inner(lambda: start_all(back_to, 2))
    is_outer(lambda: start_all(down_line, 1))

    def send_far(s, weight, c):
        xout[s, c] = combined(2 + s, 4, weight, c).astype(BF16)
        result(s, c).start()

    def settle(count):
        weight = shares(0, count)
        for c in range(PARTS):
            state[:, part(c)] += combined(0, count, weight, c)

    @is_inner
    def _():
        pick = picks(3, 4)
        for c in range(1, PARTS):
            far_rows(c, pick)
        give_all(1, 2)

    lead = PARTS // 4
    compute_half(2 + inner, 1 - inner, 1)

    @is_outer
    def _():
        for c in range(lead):
            pass_part(2, c)

    @is_inner
    def _():
        weight = shares(2, 4)
        for c in range(PARTS // 2):
            send_far(0, weight, c)

    compute_half(2 + inner, inner, 0)
    is_outer(lambda: pass_all(2, lead, 2 * lead))

    @is_inner
    def _():
        weight = shares(2, 4)
        for c in range(PARTS // 2, PARTS):
            send_far(0, weight, c)

    compute(3 - 2 * inner)

    def arrived(s, c):
        remote(fin.at[s, c], fin.at[s, c], osend.at[0, 0], orecv.at[s, c], places[2]).wait_recv()

    def send_near(weight, c):
        partial = combined(1, 2, weight, c)
        arrived(1, c)
        xout[2, c] = (partial + fin[1, c].astype(F32)).astype(BF16)
        result(2, c).start()

    @is_inner
    def _():
        near_weight = shares(1, 2)
        weight = shares(3, 4)
        lag = PARTS // 2
        for c in range(PARTS):
            send_far(1, weight, c)
            if c >= lag:
                send_near(near_weight, c - lag)
        for c in range(PARTS - lag, PARTS):
            send_near(near_weight, c)
        settle(4)

    @is_outer
    def _():
        for c in range(lead):
            down_line(3, c).start()
        pass_all(3, 0, lead)
        start_all(back_to, 1)
        compute(0, True)
        pass_all(1, 0, 0)
        settle(2)

    def write(c):
        return pltpu.make_async_copy(done.at[:, part(c)], out_ref.at[:, part(c)], dsend.at[c])

    for c in range(PARTS):
        arrived(0, c)
        done[:, part(c)] = (state[:, part(c)] + fin[0, c].astype(F32)).astype(BF16)
        write(c).start()

    for c in range(PARTS):
        write(c).wait()
    for shift in range(1, n_seq):
        share(shift).wait_send()
    for i in range(SLABS):
        slab_out(i).wait_send()
    down_out.wait_send()
    for offset in range(n_branch - 1):
        lend(offset).wait_send()
    for r in range(CHUNKS):
        rows_out(r).wait_send()
    meta_out().wait_send()

    def sent(g, f):
        remote(fwd.at[g, f - 1], fwd.at[g, f - 1], fsend.at[g, f - 1], drecv.at[0, 0], places[1]).wait_send()

    def returned(g, h):
        remote(res.at[g, h], res.at[g, h], bsend.at[g, h], brecv.at[0, 0, 0], places[1]).wait_send()

    sent(0, 1)
    for g in range(4):
        returned(g, 1)

    @is_inner
    def _():
        for g in (0, 2, 3):
            for f in ((2, 3) if g == 0 else (1, 2, 3)):
                sent(g, f)
        sent(1, 1)
        for c in range(PARTS):
            relay(c).wait_send()
            if c < early:
                relay_rows(c).wait_send()
            for s in range(3):
                result(s, c).wait_send()
        meta_relay().wait_send()

    @is_outer
    def _():
        for g in (1, 2, 3):
            returned(g, 0)
            remote(back.at[g, 0], back.at[g, 0], lsend.at[g - 1], brecv.at[0, 0, 0], places[2]).wait_send()


def run_line(listed, q, kv, residual, router_t, idt, wgu, wdn, experts, cap, n_branch, n_seq):
    rows, width = q.shape
    ff = wdn.shape[0]
    kv_width = kv.shape[1] * kv.shape[2]
    part = width // PARTS
    tall = 2 * rows
    steps = width // HEAD_SIZE * rows // tall // CHUNKS
    dma = pltpu.SemaphoreType.DMA
    return pl.pallas_call(
        functools.partial(line_kernel, experts, cap, n_branch, n_seq),
        out_shape=jax.ShapeDtypeStruct((rows, width), BF16),
        in_specs=[SMEM] + [VMEM] * 5 + [ANY, ANY],
        out_specs=ANY,
        scratch_shapes=[
            pltpu.VMEM((n_seq, rows, kv_width), BF16),
            pltpu.VMEM((n_branch - 1, rows, kv_width), BF16),
            pltpu.VMEM((n_branch - 1, rows, kv_width), BF16),
            pltpu.VMEM((CHUNKS, steps, tall, 1), F32),
            pltpu.VMEM((CHUNKS, steps, tall, 1), F32),
            pltpu.VMEM((rows, width), F32),
            pltpu.VMEM((rows, width), BF16),
            pltpu.VMEM((3, rows, width), BF16),
            pltpu.VMEM((8, rows), F32),
            pltpu.VMEM((3, 8, rows), F32),
            pltpu.VMEM((4, 2, cap, width), BF16),
            pltpu.VMEM((4, 2, cap, width), BF16),
            pltpu.VMEM((4, 3, cap, width), BF16),
            pltpu.VMEM((4, 3, cap, width), BF16),
            pltpu.VMEM((width, 2, ff), BF16),
            pltpu.VMEM((2, 2, width, ff), BF16),
            pltpu.VMEM((2, ff, width), BF16),
            pltpu.VMEM((3, PARTS, rows, part), BF16),
            pltpu.VMEM((2, PARTS, rows, part), BF16),
            pltpu.VMEM((rows, width), BF16),
            dma((n_seq - 1,)), dma((n_seq - 1,)), dma((n_branch - 1,)), dma((n_branch - 1,)),
            dma((SLABS + 1,)), dma((SLABS + 1,)), dma((SLABS + 1,)),
            dma((CHUNKS,)), dma((2, CHUNKS)), dma((PARTS + CHUNKS // 2,)), dma((PARTS + CHUNKS // 2,)), dma((2,)), dma((3,)),
            dma((4, 3)), dma((4, 2)), dma((4, 2)), dma((4, 3, PARTS)), dma((3,)), dma((3, PARTS)), dma((2, PARTS)), dma((PARTS,)),
        ],
        compiler_params=pltpu.CompilerParams(
            collective_id=2, has_side_effects=True, vmem_limit_bytes=LINE_VMEM_LIMIT
        ),
    )(listed, q, kv, residual, router_t, idt, wgu, wdn)


def on_device(
    n_branch, n_seq, queries, keyvals, residual, read_list, router, expert_ids, w_gate_up, w_down
):
    rows = queries.shape[1]
    experts = router.shape[1]
    top_count = expert_ids.shape[2]
    capacity = 2 * ((3 * rows * top_count + 4 * experts - 1) // (4 * experts))
    cap = (capacity + 15) // 16 * 16
    if n_branch == 4 and n_seq == 4 and experts == 8 and top_count == 2:
        return run_line(
            read_list.reshape(-1), queries[0], keyvals[0], residual[0], router.T, expert_ids[0].T,
            w_gate_up[0], w_down[0], experts, cap, n_branch, n_seq,
        )[None]
    kv = keyvals.reshape(rows, -1)
    wgu = jnp.swapaxes(w_gate_up[0], 0, 1)
    shifts = [
        lax.ppermute(kv, "seq", [(i, (i + step) % n_seq) for i in range(n_seq)])
        for step in range(1, n_seq)
    ]
    own = jnp.stack([kv] + shifts)
    send, state, gate, normed, meta = attend(
        read_list.reshape(-1), queries[0], own, residual[0], router.T, expert_ids[0],
        experts, experts, cap, n_branch, n_seq,
    )
    return run_experts(send, state, gate, wgu, w_down[0], experts, cap, n_seq)[None]


def solution(mesh):
    return jax.shard_map(
        functools.partial(on_device, mesh.shape["branch"], mesh.shape["seq"]),
        mesh=mesh,
        in_specs=(
            P(("rollout", "branch"), "seq", None),
            P(("rollout", "branch"), "seq", None, None),
            P(("rollout", "branch"), "seq", None),
            P(("rollout", "branch"), "seq", None),
            P(),
            P(("rollout", "branch"), "seq", None),
            P(("branch", "seq"), None, None, None),
            P(("branch", "seq"), None, None),
        ),
        out_specs=P(("rollout", "branch"), "seq", None),
        check_vma=False,
    )
```
